512 devices in a mesh: blk: 64 (over z, x_lo, core), red: 8 (over x_hi, y).
Axes of the slice: x: 4 (x_hi: 2, x_lo: 2; x = x_hi * 2 + x_lo), y: 4, z: 16, core: 2. Of those that a mesh axis runs over, the one named last changes fastest.
Arguments:
- amplitudes: float32 [16384, 6144], P('blk', 'red'), may hold values from -6 to 6
- integrals: float32 [16384, 6144], P('blk', 'red'), may hold values from -0.21875 to 0.21875
- cd_irrep: int32 [8, 768], P('red'), may hold values from 0 to 7, never falling along the last dimension, each value on 1 to 192 neighbouring positions
- ab_irrep: int32 [64, 256], P('blk'), may hold values from 0 to 7, never falling along the last dimension, each value on 1 to 64 neighbouring positions
- ij_irrep: int32 [64, 256], P('blk'), may hold values from 0 to 7, never falling along the last dimension, each value on 1 to 64 neighbouring positions
Outputs:
- ladder: float32 [4, 16384, 256], P(None, ('blk', 'red'))
The draws below stay inside these ranges and needn't reach their ends.
Inputs may be any that keep to these rules, and one draw needn't show every extreme that they name: `cd_irrep`: each row's labels never fall, every irrep 0 to 7 occurs in every row, and each irrep holds at most 192 positions of a row, exactly that many for some irrep. `ab_irrep`: each row's labels never fall, every irrep 0 to 7 occurs in every row, and each irrep holds at most 64 positions of a row, exactly that many for some irrep. `ij_irrep`: each row's labels never fall, every irrep 0 to 7 occurs in every row, and each irrep holds at most 64 positions of a row, exactly that many for some irrep.
All inputs are finite; a program needn't handle non-finite values.
Results may differ from the reference program's by a relative error of at most 0.0003.
Values sent between devices are 32-bit elements; how exact they have to be, the bound alone decides.
A program may use at most 64 MiB of HBM per device.

```python
import math
import jax
import jax.numpy as jnp
import numpy as np
from jax import lax

AB_ROWS = 256
OCC_PAIRS = 256
CD_DEV = 768
SHIFTS = 4
ROW_BLOCKS = 64
CD_PARTS = 8
CD = 6144


def shard_levels(stream_key, dims, cuts, least, top_value):
    def one(dim, shards_of):
        steps = jax.random.uniform(jax.random.fold_in(jax.random.fold_in(stream_key, 6), dim), (shards_of,), jnp.float32, least / len(cuts), top_value / len(cuts))
        return jnp.repeat(jnp.exp(steps), dims[dim] // shards_of).reshape((-1,) + (1,) * (len(dims) - dim - 1))

    factor_of = one(*cuts[0])
    for cut in cuts[1:]:
        factor_of = factor_of * one(*cut)
    return factor_of


def split_up(number_of, total, bound, lean):
    portions = [(1 << 20) // math.isqrt(rank ** lean) + 1 for rank in range(2, number_of + 1)]
    spare, counts = total - bound - (number_of - 1), [1] * (number_of - 1)
    while spare > 0:
        candidates = [i for i in range(number_of - 1) if counts[i] < bound]
        whole, left = sum([portions[i] for i in candidates]), spare
        for i in candidates:
            addition = min(bound - counts[i], max(1, left * portions[i] // whole), spare)
            counts[i] = counts[i] + addition
            spare = spare - addition
    return np.array([bound] + counts)


def ragged_sizes(key, number_of, total, bound, skew):
    if number_of == 2:
        one = jax.random.randint(key, (), max(1, total - bound), min(bound, total - 1) + 1)
        return jnp.stack([one, total - one])
    sizes = jnp.asarray(split_up(number_of, total, bound, skew), jnp.int32)
    twos = (number_of - 1) // 2
    source_of, taker = sizes[1:1 + 2 * twos:2], sizes[2:2 + 2 * twos:2]
    margin = jnp.minimum(source_of - 1, bound - taker)
    shifted = jax.random.randint(jax.random.fold_in(key, 1), (twos,), 0, 1 << 20) % (margin + 1)
    sizes = sizes.at[1:1 + 2 * twos:2].set(source_of - shifted).at[2:2 + 2 * twos:2].set(taker + shifted)
    return sizes[jax.random.permutation(jax.random.fold_in(key, 2), number_of)]


def normal_values(rng, shape, spread, reach, pieces=(), kind=jnp.bfloat16):
    entries = spread * jax.random.normal(rng, shape, jnp.float32)
    if pieces:
        entries = entries * shard_levels(rng, shape, pieces, -0.22, 0.18)
    return jnp.clip(entries, -reach, reach).astype(kind)


def setup_inputs(seed: int = 0) -> dict:
    seeds = jax.random.split(jax.random.key(seed), 6)
    return {
        "amplitudes": normal_values(seeds[0], (ROW_BLOCKS * OCC_PAIRS, CD), 1.0, 6.0, ((0, 64), (1, 8)), jnp.float32),
        "integrals": normal_values(seeds[1], (ROW_BLOCKS * AB_ROWS, CD), (CD // 8) ** -0.5, 0.21875, ((0, 64), (1, 8)), jnp.float32),
        "cd_irrep": jax.vmap(lambda own: jnp.searchsorted(jnp.cumsum(ragged_sizes(own, 8, CD_DEV, CD_DEV // 4, 1)), jnp.arange(CD_DEV), side="right"))(jax.random.split(seeds[2], CD_PARTS)).reshape((CD_PARTS, CD_DEV)).astype(jnp.int32),
        "ab_irrep": jax.vmap(lambda own: jnp.searchsorted(jnp.cumsum(ragged_sizes(own, 8, AB_ROWS, AB_ROWS // 4, 1)), jnp.arange(AB_ROWS), side="right"))(jax.random.split(seeds[3], ROW_BLOCKS)).reshape((ROW_BLOCKS, AB_ROWS)).astype(jnp.int32),
        "ij_irrep": jax.vmap(lambda own: jnp.searchsorted(jnp.cumsum(ragged_sizes(own, 8, OCC_PAIRS, OCC_PAIRS // 4, 1)), jnp.arange(OCC_PAIRS), side="right"))(jax.random.split(seeds[4], ROW_BLOCKS)).reshape((ROW_BLOCKS, OCC_PAIRS)).astype(jnp.int32),
    }


def reference(amplitudes, integrals, cd_irrep, ab_irrep, ij_irrep):
    cd_labels = cd_irrep.reshape(-1)
    amp_blocks = amplitudes.reshape(ROW_BLOCKS, OCC_PAIRS, CD)
    row_blocks = integrals.reshape(ROW_BLOCKS, AB_ROWS, CD)

    def one_block(index):
        rows = lax.dynamic_index_in_dim(row_blocks, index, 0, keepdims=False)
        row_labels = lax.dynamic_index_in_dim(ab_irrep, index, 0, keepdims=False)
        results = []
        for shift in range(SHIFTS):
            source = ((index - shift) % ROW_BLOCKS).astype(jnp.int32)
            amp_slab = lax.dynamic_index_in_dim(amp_blocks, source, 0, keepdims=False)
            slab_labels = lax.dynamic_index_in_dim(ij_irrep, source, 0, keepdims=False)
            screened = jnp.where(slab_labels[:, None] == cd_labels[None, :], amp_slab, 0.0)
            product = lax.dot_general(rows, screened, (((1,), (1,)), ((), ())), precision=lax.Precision.HIGHEST, preferred_element_type=jnp.float32)
            results.append(jnp.where(row_labels[:, None] == slab_labels[None, :], product, 0.0))
        return jnp.stack(results, 0)

    result = lax.map(one_block, jnp.arange(ROW_BLOCKS, dtype=jnp.int32))
    return jnp.transpose(result, (1, 0, 2, 3)).reshape(SHIFTS, ROW_BLOCKS * AB_ROWS, OCC_PAIRS)
```

```python
import functools

import jax
import jax.numpy as jnp
from jax import lax
from jax.experimental import pallas as pl
from jax.experimental.pallas import tpu as pltpu
from jax.sharding import PartitionSpec as P

SHIFTS = 4
MESH = pl.DeviceIdType.MESH
F32 = jnp.float32
BF16 = jnp.bfloat16
LANES = 128
HALF = 200


def lanes_below(rows):
    return lax.broadcasted_iota(jnp.int32, (rows, LANES), 1) < 64


def column_of(labels):
    return jnp.transpose(jnp.broadcast_to(labels.astype(F32), (LANES, LANES)))


def folded(ref, row, rows, own, cd_labels):
    def kept(t):
        value = ref[pl.ds(row, rows), t * LANES : (t + 1) * LANES]
        return jnp.where(own == cd_labels[:, t * LANES : (t + 1) * LANES], value, 0.0)

    f0, f1, f2 = (kept(t) + kept(t + 3) for t in range(3))
    low = lanes_below(rows)
    head = f0 + pltpu.roll(jnp.where(low, f2, f1), 64, 1)
    tail = jnp.where(low, f1, f2)
    return head, tail + pltpu.roll(tail, 64, 1)


def split(value):
    high = value.astype(BF16)
    return high, (value - high.astype(F32)).astype(BF16)


def kernel(
    n_blk, amp_hbm, int_hbm, cd_ref, ab_ref, ij_ref, out_ref,
    amp, integ, slabs, v_parts, ab_col, send, arrived, x_send, x_arrived,
    load_sem, own_send, own_recv, half_send, half_recv, fwd_send, fwd_recv,
    y_send, y_recv, xs_send, xs_recv,
):
    b, r = lax.axis_index("blk"), lax.axis_index("red")
    c = lax.rem(b, 2)
    y, x_hi = lax.rem(r, 4), r // 4
    partner = y + 4 * (1 - x_hi)

    def block(offset):
        return (lax.rem(b + offset + n_blk, n_blk), r)

    def red(k):
        return x_hi * 4 + lax.rem(y + k, 4)

    loads = [
        pltpu.make_async_copy(amp_hbm.at[pl.ds(128 * h, 128)], amp.at[pl.ds(128 * h, 128)], load_sem.at[h])
        for h in range(2)
    ] + [pltpu.make_async_copy(int_hbm, integ, load_sem.at[2])]
    for load in loads:
        load.start()

    barrier = pltpu.get_barrier_semaphore()
    for offset in (-3, -2, -1, 1):
        pl.semaphore_signal(barrier, inc=1, device_id=block(offset), device_id_type=MESH)
    for k in (1, 2, 3):
        pl.semaphore_signal(barrier, inc=1, device_id=(b, red(k)), device_id_type=MESH)
    pl.semaphore_signal(barrier, inc=1, device_id=(b, partner), device_id_type=MESH)

    cd_labels = cd_ref[...].astype(F32)
    for h in range(2):
        pair_labels = ij_ref[:, 128 * h : 128 * h + 128].astype(F32)
        own = column_of(pair_labels)
        loads[h].wait()
        tails = []
        for part in range(2):
            head, tail = folded(amp, 128 * h + 64 * part, 64, own[64 * part : 64 * part + 64], cd_labels)
            slabs[0, h, 64 * part : 64 * part + 64] = head
            tails.append(tail)
        slabs[0, h, 128:192] = jnp.where(lanes_below(64), *tails)
        slabs[0, h, 192:200] = jnp.broadcast_to(pair_labels, (8, LANES))

    pl.semaphore_wait(barrier, 8)

    def half_copy(h):
        return pltpu.make_async_remote_copy(
            src_ref=slabs.at[0, h], dst_ref=slabs.at[2 + h - c, h],
            send_sem=half_send.at[h], recv_sem=half_recv.at[1 - c],
            device_id=block(2 + h - c), device_id_type=MESH,
        )

    own_copy = pltpu.make_async_remote_copy(
        src_ref=slabs.at[0], dst_ref=slabs.at[1 + 2 * c],
        send_sem=own_send, recv_sem=own_recv,
        device_id=block(1 + 2 * c), device_id_type=MESH,
    )
    half_copy(0).start()
    half_copy(1).start()
    own_copy.start()

    def forward(i):
        return pltpu.make_async_remote_copy(
            src_ref=slabs.at[1 + i + c, c], dst_ref=slabs.at[2 + i - c, c],
            send_sem=fwd_send.at[i], recv_sem=fwd_recv.at[i],
            device_id=block(1 - 2 * c), device_id_type=MESH,
        )

    def half_arrival(i):
        return pltpu.make_async_remote_copy(
            src_ref=slabs.at[0, c], dst_ref=slabs.at[1 + i + c, c],
            send_sem=half_send.at[0], recv_sem=half_recv.at[i],
            device_id=block(2), device_id_type=MESH,
        )

    loads[2].wait()
    for h in range(2):
        own = column_of(ab_ref[:, 128 * h : 128 * h + 128])
        ab_col[128 * h : 128 * h + 128] = own
        for part in range(2):
            row = 128 * h + 64 * part
            head, tail = folded(integ, row, 64, own[64 * part : 64 * part + 64], cd_labels)
            for t, piece in enumerate((head, jnp.where(lanes_below(64), tail, 0.0))):
                high, low = split(piece)
                v_parts[row : row + 64, t * LANES : (t + 1) * LANES] = high
                v_parts[256 + row : 320 + row, t * LANES : (t + 1) * LANES] = low

    def dot(lhs, rhs):
        return lax.dot_general(lhs, rhs, (((1,), (1,)), ((), ())), preferred_element_type=F32)

    def y_copy(m, k):
        return pltpu.make_async_remote_copy(
            src_ref=send.at[m, lax.rem(y + k, 4)], dst_ref=arrived.at[m, k - 1],
            send_sem=y_send.at[m, k - 1], recv_sem=y_recv.at[m, k - 1],
            device_id=(b, red(k)), device_id_type=MESH,
        )

    def process(m):
        low = lanes_below(64)
        parts = []
        for h in range(2):
            tail = slabs[m, h, 128:192]
            parts.append(jnp.concatenate([slabs[m, h, 0:64], tail], axis=1))
            parts.append(jnp.concatenate([slabs[m, h, 64:128], pltpu.roll(tail, 64, 1)], axis=1))
        high, rest = split(jnp.concatenate(parts, axis=0))
        both = dot(v_parts[...], high)
        product = both[:256] + both[256:] + dot(v_parts[:256], rest)
        masked = jnp.zeros((256, LANES), F32)
        for h in range(2):
            mask = ab_col[...] == slabs[m, h, 192:193]
            masked = masked + jnp.where(mask, product[:, 128 * h : 128 * h + 128], 0.0)
        twice = masked + pltpu.roll(masked, 64, 1)
        low = lanes_below(16)
        for block_row in range(8):
            row = 32 * block_row
            packed = jnp.where(low, twice[row : row + 16], twice[row + 16 : row + 32])
            send[m, block_row % 4, 16 * (block_row // 4) : 16 * (block_row // 4) + 16] = packed
        for k in (1, 2, 3):
            y_copy(m, k).start()

    def x_copy(m):
        return pltpu.make_async_remote_copy(
            src_ref=x_send.at[m, 1 - x_hi], dst_ref=x_arrived.at[m],
            send_sem=xs_send.at[m], recv_sem=xs_recv.at[m],
            device_id=(b, partner), device_id_type=MESH,
        )

    def along_y(m):
        total = send[m, y]
        for k in (1, 2, 3):
            y_copy(m, k).wait_recv()
            total = total + arrived[m, k - 1]
        x_send[m, 0] = total[:16]
        x_send[m, 1] = total[16:]
        x_copy(m).start()

    def finish(m):
        x_copy(m).wait_recv()
        total = x_send[m, x_hi] + x_arrived[m]
        turned = pltpu.roll(total, 64, 1)
        low = lanes_below(16)
        first, second = jnp.where(low, total, turned), jnp.where(low, turned, total)
        rows = jnp.concatenate([first, second], axis=0)
        own = ab_col[pl.ds(pl.multiple_of(32 * r, 32), 32)]
        for h in range(2):
            mask = own == slabs[m, h, 192:193]
            out_ref[m, :, 128 * h : 128 * h + 128] = jnp.where(mask, rows, 0.0)

    first, second, third = 3 - 2 * c, 1 + c, 2 + c
    process(0)
    half_arrival(0).wait_recv()
    forward(0).start()
    half_arrival(1).wait_recv()
    forward(1).start()
    own_copy.wait_recv()
    process(first)
    along_y(0)
    forward(0).wait_recv()
    process(second)
    along_y(first)
    forward(1).wait_recv()
    process(third)
    finish(0)
    along_y(second)
    finish(first)
    along_y(third)
    finish(second)
    finish(third)

    own_copy.wait_send()
    for i in range(2):
        half_copy(i).wait_send()
        forward(i).wait_send()
    for m in range(SHIFTS):
        for k in (1, 2, 3):
            y_copy(m, k).wait_send()
        x_copy(m).wait_send()


def solution(mesh):
    n_blk = mesh.shape["blk"]

    def body(amplitudes, integrals, cd_irrep, ab_irrep, ij_irrep):
        vmem = pl.BlockSpec(memory_space=pltpu.VMEM)
        hbm = pl.BlockSpec(memory_space=pl.ANY)
        return pl.pallas_call(
            functools.partial(kernel, n_blk),
            out_shape=jax.ShapeDtypeStruct((SHIFTS, 32, 256), F32),
            in_specs=[hbm, hbm, vmem, vmem, vmem],
            out_specs=vmem,
            scratch_shapes=[
                pltpu.VMEM((256, 768), F32),
                pltpu.VMEM((256, 768), F32),
                pltpu.VMEM((SHIFTS, 2, HALF, LANES), F32),
                pltpu.VMEM((512, 256), BF16),
                pltpu.VMEM((256, LANES), F32),
                pltpu.VMEM((SHIFTS, 4, 32, LANES), F32),
                pltpu.VMEM((SHIFTS, 3, 32, LANES), F32),
                pltpu.VMEM((SHIFTS, 2, 16, LANES), F32),
                pltpu.VMEM((SHIFTS, 16, LANES), F32),
                pltpu.SemaphoreType.DMA((3,)),
                pltpu.SemaphoreType.DMA,
                pltpu.SemaphoreType.DMA,
                pltpu.SemaphoreType.DMA((2,)),
                pltpu.SemaphoreType.DMA((2,)),
                pltpu.SemaphoreType.DMA((2,)),
                pltpu.SemaphoreType.DMA((2,)),
                pltpu.SemaphoreType.DMA((SHIFTS, 3)),
                pltpu.SemaphoreType.DMA((SHIFTS, 3)),
                pltpu.SemaphoreType.DMA((SHIFTS,)),
                pltpu.SemaphoreType.DMA((SHIFTS,)),
            ],
            compiler_params=pltpu.CompilerParams(collective_id=0, has_side_effects=True),
        )(amplitudes, integrals, cd_irrep, ab_irrep, ij_irrep)

    in_specs = (P("blk", "red"), P("blk", "red"), P("red", None), P("blk", None), P("blk", None))
    out_specs = P(None, ("blk", "red"), None)
    return jax.shard_map(body, mesh=mesh, in_specs=in_specs, out_specs=out_specs, check_vma=False)
```

```python
import functools

import jax
import jax.numpy as jnp
from jax import lax
from jax.experimental import pallas as pl
from jax.experimental.pallas import tpu as pltpu
from jax.sharding import PartitionSpec as P

SHIFTS = 4
MESH = pl.DeviceIdType.MESH
F32 = jnp.float32
BF16 = jnp.bfloat16
LANES = 128
VMEM_LIMIT = 60 * 1024 * 1024
HALF = 200


def lanes_below(rows):
    return lax.broadcasted_iota(jnp.int32, (rows, LANES), 1) < 64


def column_of(labels):
    return jnp.transpose(jnp.broadcast_to(labels.astype(F32), (LANES, LANES)))


def folded(ref, row, rows, own, cd_labels):
    def kept(t):
        value = ref[pl.ds(row, rows), t * LANES : (t + 1) * LANES]
        return jnp.where(own == cd_labels[:, t * LANES : (t + 1) * LANES], value, 0.0)

    f0, f1, f2 = (kept(t) + kept(t + 3) for t in range(3))
    low = lanes_below(rows)
    head = f0 + pltpu.roll(jnp.where(low, f2, f1), 64, 1)
    tail = jnp.where(low, f1, f2)
    return head, tail + pltpu.roll(tail, 64, 1)


def split(value):
    high = value.astype(BF16)
    return high, (value - high.astype(F32)).astype(BF16)


def kernel(
    n_blk, amp_hbm, int_hbm, cd_hbm, ab_hbm, ij_hbm, out_ref,
    amp, integ, cd, ab, ij, slabs, v_parts, ab_col, send, arrived,
    load_sem, ready_sem, own_send, own_recv, half_send, half_recv, fwd_send, fwd_recv, red_send, red_recv,
):
    loads = [
        pltpu.make_async_copy(src, dst, load_sem.at[i])
        for i, (src, dst) in enumerate((
            (ij_hbm, ij),
            (cd_hbm, cd),
            (amp_hbm.at[pl.ds(0, 128)], amp.at[pl.ds(0, 128)]),
            (amp_hbm.at[pl.ds(128, 128)], amp.at[pl.ds(128, 128)]),
            (ab_hbm, ab),
            (int_hbm, integ),
        ))
    ]
    for load in loads:
        load.start()

    b, r = lax.axis_index("blk"), lax.axis_index("red")
    c = lax.rem(b, 2)
    y, x_hi = lax.rem(r, 4), r // 4

    def block(offset):
        return (lax.rem(b + offset + n_blk, n_blk), r)

    def red(x_step, y_step):
        x_to = 1 - x_hi if x_step else x_hi
        return (b, x_to * 4 + lax.rem(y + y_step, 4))

    barrier = pltpu.get_barrier_semaphore()
    for offset in (-3, -2, -1, 1):
        pl.semaphore_signal(barrier, inc=1, device_id=block(offset), device_id_type=MESH)
    for steps in ((0, 1), (0, 2), (0, 3), (1, 0)):
        pl.semaphore_signal(barrier, inc=1, device_id=red(*steps), device_id_type=MESH)

    loads[0].wait()
    loads[1].wait()
    cd_labels = cd[...].astype(F32)
    for h in range(2):
        pair_labels = ij[:, 128 * h : 128 * h + 128].astype(F32)
        own = column_of(pair_labels)
        loads[2 + h].wait()
        tails = []
        for part in range(2):
            head, tail = folded(amp, 128 * h + 64 * part, 64, own[64 * part : 64 * part + 64], cd_labels)
            slabs[0, h, 64 * part : 64 * part + 64] = head
            tails.append(tail)
        slabs[0, h, 128:192] = jnp.where(lanes_below(64), *tails)
        slabs[0, h, 192:200] = jnp.broadcast_to(pair_labels, (8, LANES))

    pl.semaphore_wait(barrier, 8)

    def half_copy(h):
        return pltpu.make_async_remote_copy(
            src_ref=slabs.at[0, h], dst_ref=slabs.at[2 + h - c, h],
            send_sem=half_send.at[h], recv_sem=half_recv.at[1 - c],
            device_id=block(2 + h - c), device_id_type=MESH,
        )

    own_copy = pltpu.make_async_remote_copy(
        src_ref=slabs.at[0], dst_ref=slabs.at[1 + 2 * c],
        send_sem=own_send, recv_sem=own_recv,
        device_id=block(1 + 2 * c), device_id_type=MESH,
    )
    half_copy(0).start()
    half_copy(1).start()
    own_copy.start()
    for y_step in (1, 2, 3):
        pl.semaphore_signal(ready_sem, inc=1, device_id=red(0, y_step), device_id_type=MESH)

    def forward(i):
        return pltpu.make_async_remote_copy(
            src_ref=slabs.at[1 + i + c, c], dst_ref=slabs.at[2 + i - c, c],
            send_sem=fwd_send.at[i], recv_sem=fwd_recv.at[i],
            device_id=block(1 - 2 * c), device_id_type=MESH,
        )

    def half_arrival(i):
        return pltpu.make_async_remote_copy(
            src_ref=slabs.at[0, c], dst_ref=slabs.at[1 + i + c, c],
            send_sem=half_send.at[0], recv_sem=half_recv.at[i],
            device_id=block(2), device_id_type=MESH,
        )

    loads[4].wait()
    loads[5].wait()
    for h in range(2):
        own = column_of(ab[:, 128 * h : 128 * h + 128])
        ab_col[128 * h : 128 * h + 128] = own
        for part in range(2):
            row = 128 * h + 64 * part
            head, tail = folded(integ, row, 64, own[64 * part : 64 * part + 64], cd_labels)
            for t, piece in enumerate((head, jnp.where(lanes_below(64), tail, 0.0))):
                high, low = split(piece)
                v_parts[row : row + 64, t * LANES : (t + 1) * LANES] = high
                v_parts[256 + row : 320 + row, t * LANES : (t + 1) * LANES] = low

    def dot(lhs, rhs):
        return lax.dot_general(lhs, rhs, (((1,), (1,)), ((), ())), preferred_element_type=F32)

    def to_peers(m):
        for x_step in range(2):
            for y_step in range(4):
                if x_step or y_step:
                    to = red(x_step, y_step)
                    pltpu.make_async_remote_copy(
                        src_ref=send.at[m, to[1]], dst_ref=arrived.at[m, 4 * x_step + y_step - 1],
                        send_sem=red_send.at[m], recv_sem=red_recv.at[m],
                        device_id=to, device_id_type=MESH,
                    ).start()

    def all_peers(m):
        return pltpu.make_async_remote_copy(
            src_ref=arrived.at[m], dst_ref=arrived.at[m],
            send_sem=red_send.at[m], recv_sem=red_recv.at[m],
            device_id=red(1, 0), device_id_type=MESH,
        )

    def process(m):
        parts = []
        for h in range(2):
            tail = slabs[m, h, 128:192]
            parts.append(jnp.concatenate([slabs[m, h, 0:64], tail], axis=1))
            parts.append(jnp.concatenate([slabs[m, h, 64:128], pltpu.roll(tail, 64, 1)], axis=1))
        high, rest = split(jnp.concatenate(parts, axis=0))
        both = dot(v_parts[...], high)
        product = both[:256] + both[256:] + dot(v_parts[:256], rest)
        masked = jnp.zeros((256, LANES), F32)
        for h in range(2):
            mask = ab_col[...] == slabs[m, h, 192:193]
            masked = masked + jnp.where(mask, product[:, 128 * h : 128 * h + 128], 0.0)
        twice = masked + pltpu.roll(masked, 64, 1)
        low = lanes_below(16)
        for block_row in range(8):
            row = 32 * block_row
            send[m, block_row] = jnp.where(low, twice[row : row + 16], twice[row + 16 : row + 32])

    def finish(m):
        all_peers(m).wait_recv()
        total = send[m, r]
        for i in range(7):
            total = total + arrived[m, i]
        turned = pltpu.roll(total, 64, 1)
        low = lanes_below(16)
        rows = jnp.concatenate([jnp.where(low, total, turned), jnp.where(low, turned, total)], axis=0)
        own = ab_col[pl.ds(pl.multiple_of(32 * r, 32), 32)]
        for h in range(2):
            mask = own == slabs[m, h, 192:193]
            out_ref[m, :, 128 * h : 128 * h + 128] = jnp.where(mask, rows, 0.0)

    first, second, third = 3 - 2 * c, 1 + c, 2 + c

    process(0)
    pl.semaphore_wait(ready_sem, 3)
    to_peers(0)

    @pl.when(c == 1)
    def _():
        own_copy.wait_recv()
        process(first)
        to_peers(first)

    half_arrival(0).wait_recv()
    forward(0).start()
    half_arrival(1).wait_recv()
    forward(1).start()
    forward(0).wait_recv()
    process(second)
    to_peers(second)
    forward(1).wait_recv()
    process(third)
    to_peers(third)

    @pl.when(c == 0)
    def _():
        own_copy.wait_recv()
        process(first)
        to_peers(first)

    finish(0)

    @pl.when(c == 1)
    def _():
        finish(first)

    finish(second)
    finish(third)

    @pl.when(c == 0)
    def _():
        finish(first)

    own_copy.wait_send()
    for i in range(2):
        half_copy(i).wait_send()
        forward(i).wait_send()
    for m in range(SHIFTS):
        all_peers(m).wait_send()


def solution(mesh):
    n_blk = mesh.shape["blk"]

    def body(amplitudes, integrals, cd_irrep, ab_irrep, ij_irrep):
        vmem = pl.BlockSpec(memory_space=pltpu.VMEM)
        hbm = pl.BlockSpec(memory_space=pltpu.HBM)
        return pl.pallas_call(
            functools.partial(kernel, n_blk),
            out_shape=jax.ShapeDtypeStruct((SHIFTS, 32, 256), F32),
            in_specs=[hbm] * 5,
            out_specs=vmem,
            scratch_shapes=[
                pltpu.VMEM((256, 768), F32),
                pltpu.VMEM((256, 768), F32),
                pltpu.VMEM((1, 768), jnp.int32),
                pltpu.VMEM((1, 256), jnp.int32),
                pltpu.VMEM((1, 256), jnp.int32),
                pltpu.VMEM((SHIFTS, 2, HALF, LANES), F32),
                pltpu.VMEM((512, 256), BF16),
                pltpu.VMEM((256, LANES), F32),
                pltpu.VMEM((SHIFTS, 8, 16, LANES), F32),
                pltpu.VMEM((SHIFTS, 7, 16, LANES), F32),
                pltpu.SemaphoreType.DMA((6,)),
                pltpu.SemaphoreType.REGULAR,
                pltpu.SemaphoreType.DMA,
                pltpu.SemaphoreType.DMA,
                pltpu.SemaphoreType.DMA((2,)),
                pltpu.SemaphoreType.DMA((2,)),
                pltpu.SemaphoreType.DMA((2,)),
                pltpu.SemaphoreType.DMA((2,)),
                pltpu.SemaphoreType.DMA((SHIFTS,)),
                pltpu.SemaphoreType.DMA((SHIFTS,)),
            ],
            compiler_params=pltpu.CompilerParams(
                collective_id=0, has_side_effects=True, vmem_limit_bytes=VMEM_LIMIT
            ),
        )(amplitudes, integrals, cd_irrep, ab_irrep, ij_irrep)

    in_specs = (P("blk", "red"), P("blk", "red"), P("red", None), P("blk", None), P("blk", None))
    out_specs = P(None, ("blk", "red"), None)
    return jax.shard_map(body, mesh=mesh, in_specs=in_specs, out_specs=out_specs, check_vma=False)
```

```python
import functools

import jax
import jax.numpy as jnp
from jax import lax
from jax.experimental import pallas as pl
from jax.experimental.pallas import tpu as pltpu
from jax.sharding import PartitionSpec as P

SHIFTS = 4
MESH = pl.DeviceIdType.MESH
F32 = jnp.float32
BF16 = jnp.bfloat16
LANES = 128
VMEM_LIMIT = 60 * 1024 * 1024
HALF = 200


def lanes_below(rows):
    return lax.broadcasted_iota(jnp.int32, (rows, LANES), 1) < 64


def column_of(labels):
    return jnp.transpose(jnp.broadcast_to(labels.astype(F32), (LANES, LANES)))


def folded(ref, row, rows, own, cd_labels):
    def kept(t):
        value = ref[pl.ds(row, rows), t * LANES : (t + 1) * LANES]
        return jnp.where(own == cd_labels[:, t * LANES : (t + 1) * LANES], value, 0.0)

    f0, f1, f2 = (kept(t) + kept(t + 3) for t in range(3))
    low = lanes_below(rows)
    head = f0 + pltpu.roll(jnp.where(low, f2, f1), 64, 1)
    tail = jnp.where(low, f1, f2)
    return head, tail + pltpu.roll(tail, 64, 1)


def split(value):
    high = value.astype(BF16)
    return high, (value - high.astype(F32)).astype(BF16)


def kernel(
    n_blk, amp_hbm, int_hbm, cd_hbm, ab_hbm, ij_hbm, out_ref,
    amp, integ, cd, ab, ij, slabs, v_parts, ab_col, send, arrived,
    load_sem, ready_sem, own_send, own_recv, half_send, half_recv, fwd_send, fwd_recv, red_send, red_recv,
):
    loads = [
        pltpu.make_async_copy(src, dst, load_sem.at[i])
        for i, (src, dst) in enumerate((
            (ij_hbm, ij),
            (cd_hbm, cd),
            (amp_hbm.at[pl.ds(0, 128)], amp.at[pl.ds(0, 128)]),
            (amp_hbm.at[pl.ds(128, 128)], amp.at[pl.ds(128, 128)]),
            (ab_hbm, ab),
            (int_hbm, integ),
        ))
    ]
    for load in loads:
        load.start()

    b, r = lax.axis_index("blk"), lax.axis_index("red")
    c = lax.rem(b, 2)
    y, x_hi = lax.rem(r, 4), r // 4

    def block(offset):
        return (lax.rem(b + offset + n_blk, n_blk), r)

    def red(x_step, y_step):
        x_to = 1 - x_hi if x_step else x_hi
        return (b, x_to * 4 + lax.rem(y + y_step, 4))

    barrier = pltpu.get_barrier_semaphore()
    for offset in (-3, -2, -1, 1):
        pl.semaphore_signal(barrier, inc=1, device_id=block(offset), device_id_type=MESH)
    for steps in ((0, 1), (0, 2), (0, 3), (1, 0)):
        pl.semaphore_signal(barrier, inc=1, device_id=red(*steps), device_id_type=MESH)

    loads[0].wait()
    loads[1].wait()
    cd_labels = cd[...].astype(F32)
    for h in range(2):
        pair_labels = ij[:, 128 * h : 128 * h + 128].astype(F32)
        own = column_of(pair_labels)
        loads[2 + h].wait()
        tails = []
        for part in range(2):
            head, tail = folded(amp, 128 * h + 64 * part, 64, own[64 * part : 64 * part + 64], cd_labels)
            slabs[0, h, 64 * part : 64 * part + 64] = head
            tails.append(tail)
        slabs[0, h, 128:192] = jnp.where(lanes_below(64), *tails)
        slabs[0, h, 192:200] = jnp.broadcast_to(pair_labels, (8, LANES))

    pl.semaphore_wait(barrier, 8)

    def half_copy(h):
        return pltpu.make_async_remote_copy(
            src_ref=slabs.at[0, h], dst_ref=slabs.at[2 + h - c, h],
            send_sem=half_send.at[h], recv_sem=half_recv.at[1 - c],
            device_id=block(2 + h - c), device_id_type=MESH,
        )

    own_copy = pltpu.make_async_remote_copy(
        src_ref=slabs.at[0], dst_ref=slabs.at[1 + 2 * c],
        send_sem=own_send, recv_sem=own_recv,
        device_id=block(1 + 2 * c), device_id_type=MESH,
    )
    half_copy(0).start()
    half_copy(1).start()
    own_copy.start()
    for y_step in (1, 2, 3):
        pl.semaphore_signal(ready_sem, inc=1, device_id=red(0, y_step), device_id_type=MESH)

    def forward(i):
        return pltpu.make_async_remote_copy(
            src_ref=slabs.at[1 + i + c, c], dst_ref=slabs.at[2 + i - c, c],
            send_sem=fwd_send.at[i], recv_sem=fwd_recv.at[i],
            device_id=block(1 - 2 * c), device_id_type=MESH,
        )

    def half_arrival(i):
        return pltpu.make_async_remote_copy(
            src_ref=slabs.at[0, c], dst_ref=slabs.at[1 + i + c, c],
            send_sem=half_send.at[0], recv_sem=half_recv.at[i],
            device_id=block(2), device_id_type=MESH,
        )

    loads[4].wait()
    loads[5].wait()
    for h in range(2):
        own = column_of(ab[:, 128 * h : 128 * h + 128])
        ab_col[128 * h : 128 * h + 128] = own
        for part in range(2):
            row = 128 * h + 64 * part
            head, tail = folded(integ, row, 64, own[64 * part : 64 * part + 64], cd_labels)
            for t, piece in enumerate((head, jnp.where(lanes_below(64), tail, 0.0))):
                high, low = split(piece)
                v_parts[row : row + 64, t * LANES : (t + 1) * LANES] = high
                v_parts[256 + row : 320 + row, t * LANES : (t + 1) * LANES] = low

    def dot(lhs, rhs):
        return lax.dot_general(lhs, rhs, (((1,), (1,)), ((), ())), preferred_element_type=F32)

    def to_peers(m):
        for x_step in range(2):
            for y_step in range(4):
                if x_step or y_step:
                    to = red(x_step, y_step)
                    pltpu.make_async_remote_copy(
                        src_ref=send.at[m, to[1]], dst_ref=arrived.at[m, 4 * x_step + y_step - 1],
                        send_sem=red_send.at[m], recv_sem=red_recv.at[m],
                        device_id=to, device_id_type=MESH,
                    ).start()

    def all_peers(m):
        return pltpu.make_async_remote_copy(
            src_ref=arrived.at[m], dst_ref=arrived.at[m],
            send_sem=red_send.at[m], recv_sem=red_recv.at[m],
            device_id=red(1, 0), device_id_type=MESH,
        )

    def process(m):
        parts = []
        for h in range(2):
            tail = slabs[m, h, 128:192]
            parts.append(jnp.concatenate([slabs[m, h, 0:64], tail], axis=1))
            parts.append(jnp.concatenate([slabs[m, h, 64:128], pltpu.roll(tail, 64, 1)], axis=1))
        high, rest = split(jnp.concatenate(parts, axis=0))
        both = dot(v_parts[...], high)
        product = both[:256] + both[256:] + dot(v_parts[:256], rest)
        masked = jnp.zeros((256, LANES), F32)
        for h in range(2):
            mask = ab_col[...] == slabs[m, h, 192:193]
            masked = masked + jnp.where(mask, product[:, 128 * h : 128 * h + 128], 0.0)
        twice = masked + pltpu.roll(masked, 64, 1)
        low = lanes_below(16)
        for block_row in range(8):
            row = 32 * block_row
            send[m, block_row] = jnp.where(low, twice[row : row + 16], twice[row + 16 : row + 32])

    def finish(m):
        all_peers(m).wait_recv()
        total = send[m, r]
        for i in range(7):
            total = total + arrived[m, i]
        turned = pltpu.roll(total, 64, 1)
        low = lanes_below(16)
        rows = jnp.concatenate([jnp.where(low, total, turned), jnp.where(low, turned, total)], axis=0)
        own = ab_col[pl.ds(pl.multiple_of(32 * r, 32), 32)]
        for h in range(2):
            mask = own == slabs[m, h, 192:193]
            out_ref[m, :, 128 * h : 128 * h + 128] = jnp.where(mask, rows, 0.0)

    first, second, third = 3 - 2 * c, 1 + c, 2 + c

    process(0)
    pl.semaphore_wait(ready_sem, 3)
    to_peers(0)

    @pl.when(c == 1)
    def _():
        own_copy.wait_recv()
        process(first)
        to_peers(first)

    half_arrival(0).wait_recv()
    forward(0).start()
    half_arrival(1).wait_recv()
    forward(1).start()
    forward(0).wait_recv()
    process(second)
    to_peers(second)
    forward(1).wait_recv()
    process(third)
    to_peers(third)

    @pl.when(c == 0)
    def _():
        own_copy.wait_recv()
        process(first)
        to_peers(first)

    finish(0)

    @pl.when(c == 1)
    def _():
        finish(first)

    finish(second)
    finish(third)

    @pl.when(c == 0)
    def _():
        finish(first)

    own_copy.wait_send()
    for i in range(2):
        half_copy(i).wait_send()
        forward(i).wait_send()
    for m in range(SHIFTS):
        all_peers(m).wait_send()


def solution(mesh):
    n_blk = mesh.shape["blk"]

    def body(amplitudes, integrals, cd_irrep, ab_irrep, ij_irrep):
        vmem = pl.BlockSpec(memory_space=pltpu.VMEM)
        hbm = pl.BlockSpec(memory_space=pltpu.HBM)
        return pl.pallas_call(
            functools.partial(kernel, n_blk),
            out_shape=pltpu.VMEM((SHIFTS, 32, 256), F32),
            in_specs=[hbm] * 5,
            out_specs=vmem,
            scratch_shapes=[
                pltpu.VMEM((256, 768), F32),
                pltpu.VMEM((256, 768), F32),
                pltpu.VMEM((1, 768), jnp.int32),
                pltpu.VMEM((1, 256), jnp.int32),
                pltpu.VMEM((1, 256), jnp.int32),
                pltpu.VMEM((SHIFTS, 2, HALF, LANES), F32),
                pltpu.VMEM((512, 256), BF16),
                pltpu.VMEM((256, LANES), F32),
                pltpu.VMEM((SHIFTS, 8, 16, LANES), F32),
                pltpu.VMEM((SHIFTS, 7, 16, LANES), F32),
                pltpu.SemaphoreType.DMA((6,)),
                pltpu.SemaphoreType.REGULAR,
                pltpu.SemaphoreType.DMA,
                pltpu.SemaphoreType.DMA,
                pltpu.SemaphoreType.DMA((2,)),
                pltpu.SemaphoreType.DMA((2,)),
                pltpu.SemaphoreType.DMA((2,)),
                pltpu.SemaphoreType.DMA((2,)),
                pltpu.SemaphoreType.DMA((SHIFTS,)),
                pltpu.SemaphoreType.DMA((SHIFTS,)),
            ],
            compiler_params=pltpu.CompilerParams(
                collective_id=0, has_side_effects=True, vmem_limit_bytes=VMEM_LIMIT
            ),
        )(amplitudes, integrals, cd_irrep, ab_irrep, ij_irrep)

    in_specs = (P("blk", "red"), P("blk", "red"), P("red", None), P("blk", None), P("blk", None))
    out_specs = P(None, ("blk", "red"), None)
    return jax.shard_map(body, mesh=mesh, in_specs=in_specs, out_specs=out_specs, check_vma=False)
```

```python
import functools

import jax
import jax.numpy as jnp
from jax import lax
from jax.experimental import pallas as pl
from jax.experimental.pallas import tpu as pltpu
from jax.sharding import PartitionSpec as P

SHIFTS = 4
MESH = pl.DeviceIdType.MESH
F32 = jnp.float32
BF16 = jnp.bfloat16
LANES = 128
VMEM_LIMIT = 60 * 1024 * 1024
HALF = 200


def lanes_below(rows):
    return lax.broadcasted_iota(jnp.int32, (rows, LANES), 1) < 64


def column_of(labels):
    return jnp.transpose(jnp.broadcast_to(labels.astype(F32), (LANES, LANES)))


def folded(ref, row, rows, own, cd_labels):
    def kept(t):
        value = ref[pl.ds(row, rows), t * LANES : (t + 1) * LANES]
        return jnp.where(own == cd_labels[:, t * LANES : (t + 1) * LANES], value, 0.0)

    f0, f1, f2 = (kept(t) + kept(t + 3) for t in range(3))
    low = lanes_below(rows)
    head = f0 + pltpu.roll(jnp.where(low, f2, f1), 64, 1)
    tail = jnp.where(low, f1, f2)
    return head, tail + pltpu.roll(tail, 64, 1)


def split(value):
    high = value.astype(BF16)
    return high, (value - high.astype(F32)).astype(BF16)


def kernel(
    n_blk, amp_hbm, int_hbm, cd_hbm, ab_hbm, ij_hbm, out_ref,
    amp, integ, cd, ab, ij, slabs, v_parts, ab_col, send, arrived,
    load_sem, ready_sem, own_send, own_recv, half_send, half_recv, fwd_send, fwd_recv,
    pass_send, pass_recv, red_send, red_recv,
):
    loads = [
        pltpu.make_async_copy(src, dst, load_sem.at[i])
        for i, (src, dst) in enumerate((
            (ij_hbm, ij),
            (cd_hbm, cd),
            (amp_hbm.at[pl.ds(0, 128)], amp.at[pl.ds(0, 128)]),
            (amp_hbm.at[pl.ds(128, 128)], amp.at[pl.ds(128, 128)]),
            (ab_hbm, ab),
            (int_hbm, integ),
        ))
    ]
    for load in loads:
        load.start()

    b, r = lax.axis_index("blk"), lax.axis_index("red")
    k = lax.rem(b, 4)
    c = lax.rem(b, 2)
    y, x_hi = lax.rem(r, 4), r // 4

    def block(offset):
        return (lax.rem(b + offset + n_blk, n_blk), r)

    def red(x_step, y_step):
        x_to = 1 - x_hi if x_step else x_hi
        return (b, x_to * 4 + lax.rem(y + y_step, 4))

    barrier = pltpu.get_barrier_semaphore()
    for offset in (-3, -2, -1, 1):
        pl.semaphore_signal(barrier, inc=1, device_id=block(offset), device_id_type=MESH)
    for steps in ((0, 1), (0, 2), (0, 3), (1, 0)):
        pl.semaphore_signal(barrier, inc=1, device_id=red(*steps), device_id_type=MESH)

    loads[0].wait()
    pair_labels = [ij[:, 128 * h : 128 * h + 128].astype(F32) for h in range(2)]
    pair_columns = [column_of(labels) for labels in pair_labels]
    loads[1].wait()
    cd_labels = cd[...].astype(F32)
    loads[2].wait()
    loads[3].wait()
    for h in range(2):
        tails = []
        for part in range(2):
            own = pair_columns[h][64 * part : 64 * part + 64]
            head, tail = folded(amp, 128 * h + 64 * part, 64, own, cd_labels)
            slabs[0, h, 64 * part : 64 * part + 64] = head
            tails.append(tail)
        slabs[0, h, 128:192] = jnp.where(lanes_below(64), *tails)
        slabs[0, h, 192:200] = jnp.broadcast_to(pair_labels[h], (8, LANES))

    pl.semaphore_wait(barrier, 8)

    def half_copy(h):
        return pltpu.make_async_remote_copy(
            src_ref=slabs.at[0, h], dst_ref=slabs.at[2 + h - c, h],
            send_sem=half_send.at[h], recv_sem=half_recv.at[1 - c],
            device_id=block(2 + h - c), device_id_type=MESH,
        )

    own_copy = pltpu.make_async_remote_copy(
        src_ref=slabs.at[0], dst_ref=slabs.at[1 + 2 * c],
        send_sem=own_send, recv_sem=own_recv,
        device_id=block(1 + 2 * c), device_id_type=MESH,
    )
    @pl.when(k != 2)
    def _():
        half_copy(0).start()
        half_copy(1).start()

    @pl.when(k != 3)
    def _():
        own_copy.start()

    for y_step in (1, 2, 3):
        pl.semaphore_signal(ready_sem, inc=1, device_id=red(0, y_step), device_id_type=MESH)

    def forward(i):
        return pltpu.make_async_remote_copy(
            src_ref=slabs.at[1 + i + c, c], dst_ref=slabs.at[2 + i - c, c],
            send_sem=fwd_send.at[i], recv_sem=fwd_recv.at[i],
            device_id=block(1 - 2 * c), device_id_type=MESH,
        )

    pass_on = pltpu.make_async_remote_copy(
        src_ref=slabs.at[1 + c, c], dst_ref=slabs.at[3, c],
        send_sem=pass_send, recv_sem=pass_recv.at[c],
        device_id=block(2 - c), device_id_type=MESH,
    )

    def passed(h):
        return pltpu.make_async_remote_copy(
            src_ref=slabs.at[0, h], dst_ref=slabs.at[3, h],
            send_sem=pass_send, recv_sem=pass_recv.at[h],
            device_id=block(-1), device_id_type=MESH,
        )

    def half_arrival(i):
        return pltpu.make_async_remote_copy(
            src_ref=slabs.at[0, c], dst_ref=slabs.at[1 + i + c, c],
            send_sem=half_send.at[0], recv_sem=half_recv.at[i],
            device_id=block(2), device_id_type=MESH,
        )

    loads[4].wait()
    loads[5].wait()
    for h in range(2):
        own = column_of(ab[:, 128 * h : 128 * h + 128])
        ab_col[128 * h : 128 * h + 128] = own
        for part in range(2):
            row = 128 * h + 64 * part
            head, tail = folded(integ, row, 64, own[64 * part : 64 * part + 64], cd_labels)
            for t, piece in enumerate((head, jnp.where(lanes_below(64), tail, 0.0))):
                high, low = split(piece)
                v_parts[row : row + 64, t * LANES : (t + 1) * LANES] = high
                v_parts[256 + row : 320 + row, t * LANES : (t + 1) * LANES] = low

    def dot(lhs, rhs):
        return lax.dot_general(lhs, rhs, (((1,), (1,)), ((), ())), preferred_element_type=F32)

    def to_peers(m):
        for x_step in (1, 0):
            for y_step in (2, 1, 3, 0):
                if x_step or y_step:
                    to = red(x_step, y_step)
                    pltpu.make_async_remote_copy(
                        src_ref=send.at[m, to[1]], dst_ref=arrived.at[m, 4 * x_step + y_step - 1],
                        send_sem=red_send.at[m], recv_sem=red_recv.at[m],
                        device_id=to, device_id_type=MESH,
                    ).start()

    def all_peers(m):
        return pltpu.make_async_remote_copy(
            src_ref=arrived.at[m], dst_ref=arrived.at[m],
            send_sem=red_send.at[m], recv_sem=red_recv.at[m],
            device_id=red(1, 0), device_id_type=MESH,
        )

    def process(m):
        parts = []
        for h in range(2):
            tail = slabs[m, h, 128:192]
            parts.append(jnp.concatenate([slabs[m, h, 0:64], tail], axis=1))
            parts.append(jnp.concatenate([slabs[m, h, 64:128], pltpu.roll(tail, 64, 1)], axis=1))
        high, rest = split(jnp.concatenate(parts, axis=0))
        both = dot(v_parts[...], high)
        product = both[:256] + both[256:] + dot(v_parts[:256], rest)
        masked = jnp.zeros((256, LANES), F32)
        for h in range(2):
            mask = ab_col[...] == slabs[m, h, 192:193]
            masked = masked + jnp.where(mask, product[:, 128 * h : 128 * h + 128], 0.0)
        twice = masked + pltpu.roll(masked, 64, 1)
        low = lanes_below(16)
        for block_row in range(8):
            row = 32 * block_row
            send[m, block_row] = jnp.where(low, twice[row : row + 16], twice[row + 16 : row + 32])

    def finish(m):
        all_peers(m).wait_recv()
        total = send[m, r]
        for i in range(7):
            total = total + arrived[m, i]
        turned = pltpu.roll(total, 64, 1)
        low = lanes_below(16)
        rows = jnp.concatenate([jnp.where(low, total, turned), jnp.where(low, turned, total)], axis=0)
        own = ab_col[pl.ds(pl.multiple_of(32 * r, 32), 32)]
        for h in range(2):
            mask = own == slabs[m, h, 192:193]
            out_ref[m, :, 128 * h : 128 * h + 128] = jnp.where(mask, rows, 0.0)

    first, second, third = 3 - 2 * c, 1 + c, 2 + c

    def shift(m):
        process(m)
        to_peers(m)

    def from_last_chip(i):
        half_arrival(i).wait_recv()
        forward(i).start()

    process(0)
    pl.semaphore_wait(ready_sem, 3)
    to_peers(0)

    @pl.when(k == 2)
    def _():
        half_copy(0).start()
        half_copy(1).start()

    @pl.when(k == 0)
    def _():
        from_last_chip(0)
        pass_on.start()
        own_copy.wait_recv()
        shift(3)
        from_last_chip(1)
        forward(0).wait_recv()
        shift(1)
        forward(1).wait_recv()
        shift(2)
        finish(0)
        finish(3)
        finish(1)
        finish(2)

    @pl.when(k == 2)
    def _():
        from_last_chip(0)
        from_last_chip(1)
        forward(0).wait_recv()
        shift(1)
        forward(1).wait_recv()
        shift(2)
        finish(0)
        passed(0).wait_recv()
        passed(1).wait_recv()
        shift(3)
        finish(1)
        finish(2)
        finish(3)

    @pl.when(c == 1)
    def _():
        own_copy.wait_recv()
        shift(1)
        from_last_chip(0)

        @pl.when(k == 1)
        def _():
            pass_on.start()

        forward(0).wait_recv()
        shift(2)
        from_last_chip(1)
        forward(1).wait_recv()
        shift(3)
        finish(0)
        finish(1)
        finish(2)
        finish(3)

    @pl.when(k != 3)
    def _():
        own_copy.wait_send()

    @pl.when(k < 2)
    def _():
        pass_on.wait_send()

    for i in range(2):
        half_copy(i).wait_send()
        forward(i).wait_send()
    for m in range(SHIFTS):
        all_peers(m).wait_send()


def solution(mesh):
    n_blk = mesh.shape["blk"]

    def body(amplitudes, integrals, cd_irrep, ab_irrep, ij_irrep):
        vmem = pl.BlockSpec(memory_space=pltpu.VMEM)
        hbm = pl.BlockSpec(memory_space=pltpu.HBM)
        return pl.pallas_call(
            functools.partial(kernel, n_blk),
            out_shape=pltpu.VMEM((SHIFTS, 32, 256), F32),
            in_specs=[hbm] * 5,
            out_specs=vmem,
            scratch_shapes=[
                pltpu.VMEM((256, 768), F32),
                pltpu.VMEM((256, 768), F32),
                pltpu.VMEM((1, 768), jnp.int32),
                pltpu.VMEM((1, 256), jnp.int32),
                pltpu.VMEM((1, 256), jnp.int32),
                pltpu.VMEM((SHIFTS, 2, HALF, LANES), F32),
                pltpu.VMEM((512, 256), BF16),
                pltpu.VMEM((256, LANES), F32),
                pltpu.VMEM((SHIFTS, 8, 16, LANES), F32),
                pltpu.VMEM((SHIFTS, 7, 16, LANES), F32),
                pltpu.SemaphoreType.DMA((6,)),
                pltpu.SemaphoreType.REGULAR,
                pltpu.SemaphoreType.DMA,
                pltpu.SemaphoreType.DMA,
                pltpu.SemaphoreType.DMA((2,)),
                pltpu.SemaphoreType.DMA((2,)),
                pltpu.SemaphoreType.DMA((2,)),
                pltpu.SemaphoreType.DMA((2,)),
                pltpu.SemaphoreType.DMA,
                pltpu.SemaphoreType.DMA((2,)),
                pltpu.SemaphoreType.DMA((SHIFTS,)),
                pltpu.SemaphoreType.DMA((SHIFTS,)),
            ],
            compiler_params=pltpu.CompilerParams(
                collective_id=0, has_side_effects=True, vmem_limit_bytes=VMEM_LIMIT
            ),
        )(amplitudes, integrals, cd_irrep, ab_irrep, ij_irrep)

    in_specs = (P("blk", "red"), P("blk", "red"), P("red", None), P("blk", None), P("blk", None))
    out_specs = P(None, ("blk", "red"), None)
    return jax.shard_map(body, mesh=mesh, in_specs=in_specs, out_specs=out_specs, check_vma=False)
```

```python
import functools

import jax
import jax.numpy as jnp
from jax import lax
from jax.experimental import pallas as pl
from jax.experimental.pallas import tpu as pltpu
from jax.sharding import PartitionSpec as P

SHIFTS = 4
MESH = pl.DeviceIdType.MESH
F32 = jnp.float32
BF16 = jnp.bfloat16
LANES = 128
VMEM_LIMIT = 60 * 1024 * 1024
CUTS = ((0, 104), (104, 96))
HALF = 200


def lanes_below(rows):
    return lax.broadcasted_iota(jnp.int32, (rows, LANES), 1) < 64


def column_of(labels):
    return jnp.transpose(jnp.broadcast_to(labels.astype(F32), (LANES, LANES)))


def folded(ref, row, rows, own, cd_labels):
    def kept(t):
        value = ref[pl.ds(row, rows), t * LANES : (t + 1) * LANES]
        return jnp.where(own == cd_labels[:, t * LANES : (t + 1) * LANES], value, 0.0)

    f0, f1, f2 = (kept(t) + kept(t + 3) for t in range(3))
    low = lanes_below(rows)
    head = f0 + pltpu.roll(jnp.where(low, f2, f1), 64, 1)
    tail = jnp.where(low, f1, f2)
    return head, tail + pltpu.roll(tail, 64, 1)


def split(value):
    high = value.astype(BF16)
    return high, (value - high.astype(F32)).astype(BF16)


def kernel(
    n_blk, amp_hbm, int_hbm, cd_hbm, ab_hbm, ij_hbm, out_ref,
    amp, integ, cd, ab, ij, slabs, v_parts, ab_col, send, arrived,
    load_sem, ready_sem, own_send, own_recv, half_send, half_recv, fwd_send, fwd_recv,
    pass_send, pass_recv, red_send, red_recv,
):
    loads = [
        pltpu.make_async_copy(src, dst, load_sem.at[i])
        for i, (src, dst) in enumerate((
            (ij_hbm, ij),
            (cd_hbm, cd),
            (amp_hbm.at[pl.ds(0, 128)], amp.at[pl.ds(0, 128)]),
            (amp_hbm.at[pl.ds(128, 128)], amp.at[pl.ds(128, 128)]),
            (ab_hbm, ab),
            (int_hbm, integ),
        ))
    ]
    for load in loads[:4]:
        load.start()

    b, r = lax.axis_index("blk"), lax.axis_index("red")
    k = lax.rem(b, 4)
    c = lax.rem(b, 2)
    y, x_hi = lax.rem(r, 4), r // 4

    def block(offset):
        return (lax.rem(b + offset + n_blk, n_blk), r)

    def red(x_step, y_step):
        x_to = 1 - x_hi if x_step else x_hi
        return (b, x_to * 4 + lax.rem(y + y_step, 4))

    barrier = pltpu.get_barrier_semaphore()
    for offset in (-3, -2, -1, 1):
        pl.semaphore_signal(barrier, inc=1, device_id=block(offset), device_id_type=MESH)
    for steps in ((0, 1), (0, 2), (0, 3), (1, 0)):
        pl.semaphore_signal(barrier, inc=1, device_id=red(*steps), device_id_type=MESH)

    loads[0].wait()
    pair_labels = [ij[:, 128 * h : 128 * h + 128].astype(F32) for h in range(2)]
    pair_columns = [column_of(labels) for labels in pair_labels]
    loads[1].wait()
    cd_labels = cd[...].astype(F32)
    for h in range(2):
        loads[2 + h].wait()
        tails = []
        for part in range(2):
            own = pair_columns[h][64 * part : 64 * part + 64]
            head, tail = folded(amp, 128 * h + 64 * part, 64, own, cd_labels)
            slabs[0, h, 64 * part : 64 * part + 64] = head
            tails.append(tail)
        slabs[0, h, 128:192] = jnp.where(lanes_below(64), *tails)
        slabs[0, h, 192:200] = jnp.broadcast_to(pair_labels[h], (8, LANES))
    loads[4].start()
    loads[5].start()

    pl.semaphore_wait(barrier, 8)

    def chunk(m, h, q):
        return slabs.at[m, h, pl.ds(*CUTS[q])]

    def half_copy(h, q):
        return pltpu.make_async_remote_copy(
            src_ref=chunk(0, h, q), dst_ref=chunk(2 + h - c, h, q),
            send_sem=half_send.at[h, q], recv_sem=half_recv.at[1 - c, q],
            device_id=block(2 + h - c), device_id_type=MESH,
        )

    def send_halves():
        for h in range(2):
            for q in range(2):
                half_copy(h, q).start()

    own_copy = pltpu.make_async_remote_copy(
        src_ref=slabs.at[0], dst_ref=slabs.at[1 + 2 * c],
        send_sem=own_send, recv_sem=own_recv,
        device_id=block(1 + 2 * c), device_id_type=MESH,
    )
    @pl.when(k != 2)
    def _():
        send_halves()

    @pl.when(k != 3)
    def _():
        own_copy.start()

    for y_step in (1, 2, 3):
        pl.semaphore_signal(ready_sem, inc=1, device_id=red(0, y_step), device_id_type=MESH)

    def forward(i, q):
        return pltpu.make_async_remote_copy(
            src_ref=chunk(1 + i + c, c, q), dst_ref=chunk(2 + i - c, c, q),
            send_sem=fwd_send.at[i, q], recv_sem=fwd_recv.at[i, q],
            device_id=block(1 - 2 * c), device_id_type=MESH,
        )

    def forwarded(i):
        for q in range(2):
            forward(i, q).wait_recv()

    def pass_on(q):
        return pltpu.make_async_remote_copy(
            src_ref=chunk(1 + c, c, q), dst_ref=chunk(3, c, q),
            send_sem=pass_send.at[q], recv_sem=pass_recv.at[c, q],
            device_id=block(2 - c), device_id_type=MESH,
        )

    def passed(h, q):
        return pltpu.make_async_remote_copy(
            src_ref=chunk(0, h, q), dst_ref=chunk(3, h, q),
            send_sem=pass_send.at[q], recv_sem=pass_recv.at[h, q],
            device_id=block(-1), device_id_type=MESH,
        )

    def half_arrival(i, q):
        return pltpu.make_async_remote_copy(
            src_ref=chunk(0, c, q), dst_ref=chunk(1 + i + c, c, q),
            send_sem=half_send.at[0, q], recv_sem=half_recv.at[i, q],
            device_id=block(2), device_id_type=MESH,
        )

    def from_last_chip(i, hand_on=False):
        for q in range(2):
            half_arrival(i, q).wait_recv()
            if hand_on:
                pass_on(q).start()
            forward(i, q).start()

    loads[4].wait()
    loads[5].wait()
    for h in range(2):
        own = column_of(ab[:, 128 * h : 128 * h + 128])
        ab_col[128 * h : 128 * h + 128] = own
        for part in range(2):
            row = 128 * h + 64 * part
            head, tail = folded(integ, row, 64, own[64 * part : 64 * part + 64], cd_labels)
            for t, piece in enumerate((head, jnp.where(lanes_below(64), tail, 0.0))):
                high, low = split(piece)
                v_parts[row : row + 64, t * LANES : (t + 1) * LANES] = high
                v_parts[256 + row : 320 + row, t * LANES : (t + 1) * LANES] = low

    def dot(lhs, rhs):
        return lax.dot_general(lhs, rhs, (((1,), (1,)), ((), ())), preferred_element_type=F32)

    def to_peers(m):
        for x_step in (1, 0):
            for y_step in (2, 1, 3, 0):
                if x_step or y_step:
                    to = red(x_step, y_step)
                    pltpu.make_async_remote_copy(
                        src_ref=send.at[m, to[1]], dst_ref=arrived.at[m, 4 * x_step + y_step - 1],
                        send_sem=red_send.at[m], recv_sem=red_recv.at[m],
                        device_id=to, device_id_type=MESH,
                    ).start()

    def all_peers(m):
        return pltpu.make_async_remote_copy(
            src_ref=arrived.at[m], dst_ref=arrived.at[m],
            send_sem=red_send.at[m], recv_sem=red_recv.at[m],
            device_id=red(1, 0), device_id_type=MESH,
        )

    def process(m):
        parts = []
        for h in range(2):
            tail = slabs[m, h, 128:192]
            parts.append(jnp.concatenate([slabs[m, h, 0:64], tail], axis=1))
            parts.append(jnp.concatenate([slabs[m, h, 64:128], pltpu.roll(tail, 64, 1)], axis=1))
        high, rest = split(jnp.concatenate(parts, axis=0))
        both = dot(v_parts[...], high)
        product = both[:256] + both[256:] + dot(v_parts[:256], rest)
        masked = jnp.zeros((256, LANES), F32)
        for h in range(2):
            mask = ab_col[...] == slabs[m, h, 192:193]
            masked = masked + jnp.where(mask, product[:, 128 * h : 128 * h + 128], 0.0)
        twice = masked + pltpu.roll(masked, 64, 1)
        low = lanes_below(16)
        for block_row in range(8):
            row = 32 * block_row
            send[m, block_row] = jnp.where(low, twice[row : row + 16], twice[row + 16 : row + 32])

    def finish(m):
        all_peers(m).wait_recv()
        total = send[m, r]
        for i in range(7):
            total = total + arrived[m, i]
        turned = pltpu.roll(total, 64, 1)
        low = lanes_below(16)
        rows = jnp.concatenate([jnp.where(low, total, turned), jnp.where(low, turned, total)], axis=0)
        own = ab_col[pl.ds(pl.multiple_of(32 * r, 32), 32)]
        for h in range(2):
            mask = own == slabs[m, h, 192:193]
            out_ref[m, :, 128 * h : 128 * h + 128] = jnp.where(mask, rows, 0.0)

    first, second, third = 3 - 2 * c, 1 + c, 2 + c

    def shift(m):
        process(m)
        to_peers(m)

    process(0)

    @pl.when(k == 2)
    def _():
        send_halves()

    pl.semaphore_wait(ready_sem, 3)
    to_peers(0)

    @pl.when(k == 0)
    def _():
        from_last_chip(0, hand_on=True)
        own_copy.wait_recv()
        shift(3)
        from_last_chip(1)
        forwarded(0)
        shift(1)
        forwarded(1)
        shift(2)
        finish(0)
        finish(3)
        finish(1)
        finish(2)

    @pl.when(k == 2)
    def _():
        from_last_chip(0)
        from_last_chip(1)
        forwarded(0)
        shift(1)
        forwarded(1)
        shift(2)
        finish(0)
        for h in range(2):
            for q in range(2):
                passed(h, q).wait_recv()
        shift(3)
        finish(1)
        finish(2)
        finish(3)

    @pl.when(c == 1)
    def _():
        own_copy.wait_recv()
        shift(1)

        @pl.when(k == 1)
        def _():
            from_last_chip(0, hand_on=True)

        @pl.when(k == 3)
        def _():
            from_last_chip(0)

        forwarded(0)
        shift(2)
        from_last_chip(1)
        forwarded(1)
        shift(3)
        finish(0)
        finish(1)
        finish(2)
        finish(3)

    @pl.when(k != 3)
    def _():
        own_copy.wait_send()

    @pl.when(k < 2)
    def _():
        for q in range(2):
            pass_on(q).wait_send()

    for i in range(2):
        for q in range(2):
            half_copy(i, q).wait_send()
            forward(i, q).wait_send()
    for m in range(SHIFTS):
        all_peers(m).wait_send()


def solution(mesh):
    n_blk = mesh.shape["blk"]

    def body(amplitudes, integrals, cd_irrep, ab_irrep, ij_irrep):
        vmem = pl.BlockSpec(memory_space=pltpu.VMEM)
        hbm = pl.BlockSpec(memory_space=pltpu.HBM)
        return pl.pallas_call(
            functools.partial(kernel, n_blk),
            out_shape=pltpu.VMEM((SHIFTS, 32, 256), F32),
            in_specs=[hbm] * 5,
            out_specs=vmem,
            scratch_shapes=[
                pltpu.VMEM((256, 768), F32),
                pltpu.VMEM((256, 768), F32),
                pltpu.VMEM((1, 768), jnp.int32),
                pltpu.VMEM((1, 256), jnp.int32),
                pltpu.VMEM((1, 256), jnp.int32),
                pltpu.VMEM((SHIFTS, 2, HALF, LANES), F32),
                pltpu.VMEM((512, 256), BF16),
                pltpu.VMEM((256, LANES), F32),
                pltpu.VMEM((SHIFTS, 8, 16, LANES), F32),
                pltpu.VMEM((SHIFTS, 7, 16, LANES), F32),
                pltpu.SemaphoreType.DMA((6,)),
                pltpu.SemaphoreType.REGULAR,
                pltpu.SemaphoreType.DMA,
                pltpu.SemaphoreType.DMA,
                pltpu.SemaphoreType.DMA((2, 2)),
                pltpu.SemaphoreType.DMA((2, 2)),
                pltpu.SemaphoreType.DMA((2, 2)),
                pltpu.SemaphoreType.DMA((2, 2)),
                pltpu.SemaphoreType.DMA((2,)),
                pltpu.SemaphoreType.DMA((2, 2)),
                pltpu.SemaphoreType.DMA((SHIFTS,)),
                pltpu.SemaphoreType.DMA((SHIFTS,)),
            ],
            compiler_params=pltpu.CompilerParams(
                collective_id=0, has_side_effects=True, vmem_limit_bytes=VMEM_LIMIT
            ),
        )(amplitudes, integrals, cd_irrep, ab_irrep, ij_irrep)

    in_specs = (P("blk", "red"), P("blk", "red"), P("red", None), P("blk", None), P("blk", None))
    out_specs = P(None, ("blk", "red"), None)
    return jax.shard_map(body, mesh=mesh, in_specs=in_specs, out_specs=out_specs, check_vma=False)
```

```python
import functools

import jax
import jax.numpy as jnp
from jax import lax
from jax.experimental import pallas as pl
from jax.experimental.pallas import tpu as pltpu
from jax.sharding import PartitionSpec as P

SHIFTS = 4
MESH = pl.DeviceIdType.MESH
F32 = jnp.float32
BF16 = jnp.bfloat16
LANES = 128
NEAR = ((0, 1), (0, 3), (1, 0))
VMEM_LIMIT = 60 * 1024 * 1024
CUTS = ((0, 96), (96, 96))
HALF = 192


def lanes_below(rows):
    return lax.broadcasted_iota(jnp.int32, (rows, LANES), 1) < 64


def column_of(labels):
    return jnp.transpose(jnp.broadcast_to(labels.astype(F32), (LANES, LANES)))


def folded(ref, row, rows, own, cd_labels):
    def kept(t):
        value = ref[pl.ds(row, rows), t * LANES : (t + 1) * LANES]
        return jnp.where(own == cd_labels[:, t * LANES : (t + 1) * LANES], value, 0.0)

    f0, f1, f2 = (kept(t) + kept(t + 3) for t in range(3))
    low = lanes_below(rows)
    head = f0 + pltpu.roll(jnp.where(low, f2, f1), 64, 1)
    tail = jnp.where(low, f1, f2)
    return head, tail + pltpu.roll(tail, 64, 1)


def split(value):
    high = value.astype(BF16)
    return high, (value - high.astype(F32)).astype(BF16)


def kernel(
    n_blk, amp_hbm, int_hbm, cd_hbm, ab_hbm, ij_hbm, out_ref,
    amp, integ, cd, ab, labels, slabs, v_parts, ab_col, send, arrived,
    load_sem, near_sem, far_sem, label_send, label_recv, slab_send, own_recv, half_recv, fwd_recv, pass_recv,
    red_send, red_recv,
):
    loads = [
        pltpu.make_async_copy(src, dst, load_sem.at[i])
        for i, (src, dst) in enumerate((
            (ij_hbm, labels.at[0]),
            (cd_hbm, cd),
            (amp_hbm.at[pl.ds(0, 128)], amp.at[pl.ds(0, 128)]),
            (amp_hbm.at[pl.ds(128, 128)], amp.at[pl.ds(128, 128)]),
            (ab_hbm, ab),
            (int_hbm, integ),
        ))
    ]
    for load in loads[:4]:
        load.start()

    b, r = lax.axis_index("blk"), lax.axis_index("red")
    k = lax.rem(b, 4)
    c = lax.rem(b, 2)
    y, x_hi = lax.rem(r, 4), r // 4

    def block(offset):
        return (lax.rem(b + offset + n_blk, n_blk), r)

    def red(x_step, y_step):
        x_to = 1 - x_hi if x_step else x_hi
        return (b, x_to * 4 + lax.rem(y + y_step, 4))

    barrier = pltpu.get_barrier_semaphore()
    for offset in (-3, -2, -1, 1):
        pl.semaphore_signal(barrier, inc=1, device_id=block(offset), device_id_type=MESH)
    for steps in NEAR:
        pl.semaphore_signal(barrier, inc=1, device_id=red(*steps), device_id_type=MESH)

    def label_copy(m):
        return pltpu.make_async_remote_copy(
            src_ref=labels.at[0], dst_ref=labels.at[m],
            send_sem=label_send, recv_sem=label_recv.at[m - 1],
            device_id=block(m), device_id_type=MESH,
        )

    def chunk(m, h, q):
        return slabs.at[2 * m + h, pl.ds(*CUTS[q])]

    def half_copy(h, q):
        return pltpu.make_async_remote_copy(
            src_ref=chunk(0, h, q), dst_ref=chunk(2 + h - c, h, q),
            send_sem=slab_send, recv_sem=half_recv.at[1 - c, q],
            device_id=block(2 + h - c), device_id_type=MESH,
        )

    def send_half(h):
        for q in range(2):
            half_copy(h, q).start()

    own_copy = pltpu.make_async_remote_copy(
        src_ref=slabs.at[pl.ds(0, 2)], dst_ref=slabs.at[pl.ds(2 + 4 * c, 2)],
        send_sem=slab_send, recv_sem=own_recv,
        device_id=block(1 + 2 * c), device_id_type=MESH,
    )
    loads[0].wait()
    pair_labels = [labels[0, :, 128 * h : 128 * h + 128] for h in range(2)]
    pair_columns = [column_of(row) for row in pair_labels]
    loads[1].wait()
    cd_labels = cd[...].astype(F32)
    loads[2].wait()
    for h in range(2):
        tails = []
        for part in range(2):
            own = pair_columns[h][64 * part : 64 * part + 64]
            head, tail = folded(amp, 128 * h + 64 * part, 64, own, cd_labels)
            slabs[h, 64 * part : 64 * part + 64] = head
            tails.append(tail)
        slabs[h, 128:192] = jnp.where(lanes_below(64), *tails)
        if h == 0:
            loads[3].wait()
            loads[4].start()
            loads[5].start()
            pl.semaphore_wait(barrier, 7)
            for m in (1, 2, 3):
                label_copy(m).start()

        @pl.when(k != 2)
        def _(h=h):
            send_half(h)

    @pl.when(k != 3)
    def _():
        own_copy.start()

    for steps in NEAR:
        pl.semaphore_signal(near_sem, inc=1, device_id=red(*steps), device_id_type=MESH)

    def forward(i, q):
        return pltpu.make_async_remote_copy(
            src_ref=chunk(1 + i + c, c, q), dst_ref=chunk(2 + i - c, c, q),
            send_sem=slab_send, recv_sem=fwd_recv.at[i],
            device_id=block(1 - 2 * c), device_id_type=MESH,
        )

    def forwarded(i):
        pltpu.make_async_remote_copy(
            src_ref=slabs.at[0], dst_ref=slabs.at[0],
            send_sem=slab_send, recv_sem=fwd_recv.at[i],
            device_id=block(1 - 2 * c), device_id_type=MESH,
        ).wait_recv()

    def pass_on(q):
        return pltpu.make_async_remote_copy(
            src_ref=chunk(1 + c, c, q), dst_ref=chunk(3, c, q),
            send_sem=slab_send, recv_sem=pass_recv,
            device_id=block(2 - c), device_id_type=MESH,
        )

    def all_slab_copies(halves):
        return pltpu.make_async_remote_copy(
            src_ref=slabs.at[pl.ds(0, halves)], dst_ref=slabs.at[pl.ds(0, halves)],
            send_sem=slab_send, recv_sem=pass_recv,
            device_id=block(2), device_id_type=MESH,
        )

    def half_arrival(i, q):
        return pltpu.make_async_remote_copy(
            src_ref=chunk(0, c, q), dst_ref=chunk(1 + i + c, c, q),
            send_sem=slab_send, recv_sem=half_recv.at[i, q],
            device_id=block(2), device_id_type=MESH,
        )

    def from_last_chip(i, hand_on=False):
        for q in range(2):
            half_arrival(i, q).wait_recv()
            if hand_on:
                pass_on(q).start()
            forward(i, q).start()

    loads[4].wait()
    loads[5].wait()
    for h in range(2):
        own = column_of(ab[:, 128 * h : 128 * h + 128])
        ab_col[128 * h : 128 * h + 128] = own
        for part in range(2):
            row = 128 * h + 64 * part
            head, tail = folded(integ, row, 64, own[64 * part : 64 * part + 64], cd_labels)
            for t, piece in enumerate((head, jnp.where(lanes_below(64), tail, 0.0))):
                high, low = split(piece)
                for place, value in ((t, high), (t + 2, low), (t + 4, high)):
                    v_parts[row : row + 64, place * LANES : (place + 1) * LANES] = value

    def dot(lhs, rhs):
        return lax.dot_general(lhs, rhs, (((1,), (1,)), ((), ())), preferred_element_type=F32)

    def to_peers(m):
        for x_step in (1, 0):
            for y_step in (2, 1, 3, 0):
                if x_step or y_step:
                    to = red(x_step, y_step)
                    pltpu.make_async_remote_copy(
                        src_ref=send.at[m, to[1]], dst_ref=arrived.at[m, 4 * x_step + y_step - 1],
                        send_sem=red_send, recv_sem=red_recv.at[m],
                        device_id=to, device_id_type=MESH,
                    ).start()

    def all_peers(m):
        return pltpu.make_async_remote_copy(
            src_ref=arrived.at[m], dst_ref=arrived.at[m],
            send_sem=red_send, recv_sem=red_recv.at[m],
            device_id=red(1, 0), device_id_type=MESH,
        )

    def process(m):
        parts = []
        for h in range(2):
            tail = slabs[2 * m + h, 128:192]
            parts.append(jnp.concatenate([slabs[2 * m + h, 0:64], tail], axis=1))
            parts.append(jnp.concatenate([slabs[2 * m + h, 64:128], pltpu.roll(tail, 64, 1)], axis=1))
        high, rest = split(jnp.concatenate(parts, axis=0))
        product = dot(v_parts[...], jnp.concatenate([high, high, rest], axis=1))
        masked = jnp.zeros((256, LANES), F32)
        for h in range(2):
            mask = ab_col[...] == labels[m, :, 128 * h : 128 * h + 128].astype(F32)
            masked = masked + jnp.where(mask, product[:, 128 * h : 128 * h + 128], 0.0)
        twice = masked + pltpu.roll(masked, 64, 1)
        low = lanes_below(16)
        for block_row in range(8):
            row = 32 * block_row
            send[m, block_row] = jnp.where(low, twice[row : row + 16], twice[row + 16 : row + 32])

    def finish(m):
        all_peers(m).wait_recv()
        total = send[m, r]
        for i in range(7):
            total = total + arrived[m, i]
        turned = pltpu.roll(total, 64, 1)
        low = lanes_below(16)
        rows = jnp.concatenate([jnp.where(low, total, turned), jnp.where(low, turned, total)], axis=0)
        own = ab_col[pl.ds(pl.multiple_of(32 * r, 32), 32)]
        for h in range(2):
            mask = own == labels[m, :, 128 * h : 128 * h + 128].astype(F32)
            out_ref[m, :, 128 * h : 128 * h + 128] = jnp.where(mask, rows, 0.0)

    first, second, third = 3 - 2 * c, 1 + c, 2 + c

    def shift(m):
        label_copy(m).wait_recv()
        process(m)
        to_peers(m)

    process(0)

    @pl.when(k == 2)
    def _():
        send_half(0)
        send_half(1)

    pl.semaphore_wait(near_sem, 3)
    pl.semaphore_signal(far_sem, inc=1, device_id=red(0, 3), device_id_type=MESH)
    pl.semaphore_wait(far_sem, 1)
    to_peers(0)

    @pl.when(k == 0)
    def _():
        from_last_chip(0, hand_on=True)
        own_copy.wait_recv()
        shift(3)
        from_last_chip(1)
        forwarded(0)
        shift(1)
        forwarded(1)
        shift(2)
        finish(0)
        finish(3)
        finish(1)
        finish(2)

    @pl.when(k == 2)
    def _():
        from_last_chip(0)
        from_last_chip(1)
        forwarded(0)
        shift(1)
        forwarded(1)
        shift(2)
        finish(0)
        all_slab_copies(2).wait_recv()
        shift(3)
        finish(1)
        finish(2)
        finish(3)

    @pl.when(c == 1)
    def _():
        own_copy.wait_recv()
        shift(1)

        @pl.when(k == 1)
        def _():
            from_last_chip(0, hand_on=True)

        @pl.when(k == 3)
        def _():
            from_last_chip(0)

        forwarded(0)
        shift(2)
        from_last_chip(1)
        forwarded(1)
        shift(3)
        finish(0)
        finish(1)
        finish(2)
        finish(3)

    for halves, blocks in ((7, k < 2), (6, k == 2), (4, k == 3)):
        @pl.when(blocks)
        def _(halves=halves):
            all_slab_copies(halves).wait_send()

    pltpu.make_async_remote_copy(
        src_ref=labels.at[pl.ds(1, 3)], dst_ref=labels.at[pl.ds(1, 3)],
        send_sem=label_send, recv_sem=label_recv.at[0],
        device_id=block(1), device_id_type=MESH,
    ).wait_send()
    pltpu.make_async_remote_copy(
        src_ref=arrived, dst_ref=arrived,
        send_sem=red_send, recv_sem=red_recv.at[0],
        device_id=red(1, 0), device_id_type=MESH,
    ).wait_send()


def solution(mesh):
    n_blk = mesh.shape["blk"]

    def body(amplitudes, integrals, cd_irrep, ab_irrep, ij_irrep):
        vmem = pl.BlockSpec(memory_space=pltpu.VMEM)
        hbm = pl.BlockSpec(memory_space=pltpu.HBM)
        return pl.pallas_call(
            functools.partial(kernel, n_blk),
            out_shape=pltpu.VMEM((SHIFTS, 32, 256), F32),
            in_specs=[hbm] * 5,
            out_specs=vmem,
            scratch_shapes=[
                pltpu.VMEM((256, 768), F32),
                pltpu.VMEM((256, 768), F32),
                pltpu.VMEM((1, 768), jnp.int32),
                pltpu.VMEM((1, 256), jnp.int32),
                pltpu.VMEM((SHIFTS, 1, 256), jnp.int32),
                pltpu.VMEM((2 * SHIFTS, HALF, LANES), F32),
                pltpu.VMEM((256, 768), BF16),
                pltpu.VMEM((256, LANES), F32),
                pltpu.VMEM((SHIFTS, 8, 16, LANES), F32),
                pltpu.VMEM((SHIFTS, 7, 16, LANES), F32),
                pltpu.SemaphoreType.DMA((6,)),
                pltpu.SemaphoreType.REGULAR,
                pltpu.SemaphoreType.REGULAR,
                pltpu.SemaphoreType.DMA,
                pltpu.SemaphoreType.DMA((3,)),
                pltpu.SemaphoreType.DMA,
                pltpu.SemaphoreType.DMA,
                pltpu.SemaphoreType.DMA((2, 2)),
                pltpu.SemaphoreType.DMA((2,)),
                pltpu.SemaphoreType.DMA,
                pltpu.SemaphoreType.DMA,
                pltpu.SemaphoreType.DMA((SHIFTS,)),
            ],
            compiler_params=pltpu.CompilerParams(
                collective_id=0, has_side_effects=True, vmem_limit_bytes=VMEM_LIMIT
            ),
        )(amplitudes, integrals, cd_irrep, ab_irrep, ij_irrep)

    in_specs = (P("blk", "red"), P("blk", "red"), P("red", None), P("blk", None), P("blk", None))
    out_specs = P(None, ("blk", "red"), None)
    return jax.shard_map(body, mesh=mesh, in_specs=in_specs, out_specs=out_specs, check_vma=False)
```

```python
import functools

import jax
import jax.numpy as jnp
from jax import lax
from jax.experimental import pallas as pl
from jax.experimental.pallas import tpu as pltpu
from jax.sharding import PartitionSpec as P

SHIFTS = 4
MESH = pl.DeviceIdType.MESH
F32 = jnp.float32
BF16 = jnp.bfloat16
LANES = 128
NEAR = ((0, 1), (0, 3), (1, 0))
VMEM_LIMIT = 60 * 1024 * 1024
CUTS = ((0, 96), (96, 96))
HALF = 192


def lanes_below(rows):
    return lax.broadcasted_iota(jnp.int32, (rows, LANES), 1) < 64


def column_of(labels):
    return jnp.transpose(jnp.broadcast_to(labels.astype(F32), (LANES, LANES)))


def folded(ref, row, rows, own, cd_labels):
    def kept(t):
        value = ref[pl.ds(row, rows), t * LANES : (t + 1) * LANES]
        return jnp.where(own == cd_labels[:, t * LANES : (t + 1) * LANES], value, 0.0)

    f0, f1, f2 = (kept(t) + kept(t + 3) for t in range(3))
    low = lanes_below(rows)
    head = f0 + pltpu.roll(jnp.where(low, f2, f1), 64, 1)
    tail = jnp.where(low, f1, f2)
    return head, tail + pltpu.roll(tail, 64, 1)


def split(value):
    high = value.astype(BF16)
    return high, (value - high.astype(F32)).astype(BF16)


def kernel(
    n_blk, amp_hbm, int_hbm, cd_hbm, ab_hbm, ij_hbm, out_ref,
    amp, integ, cd, ab, labels, slabs, v_parts, ab_col, send, arrived,
    load_sem, reply_sem, near_sem, far_sem, label_send, label_recv, slab_send, own_recv, half_recv, fwd_recv, pass_recv,
    red_send, red_recv,
):
    loads = [
        pltpu.make_async_copy(src, dst, load_sem.at[i])
        for i, (src, dst) in enumerate((
            (ij_hbm, labels.at[0]),
            (cd_hbm, cd),
            (amp_hbm.at[pl.ds(0, 128)], amp.at[pl.ds(0, 128)]),
            (amp_hbm.at[pl.ds(128, 128)], amp.at[pl.ds(128, 128)]),
            (ab_hbm, ab),
            (int_hbm, integ),
        ))
    ]
    for load in loads[:3]:
        load.start()

    b, r = lax.axis_index("blk"), lax.axis_index("red")
    k = lax.rem(b, 4)
    c = lax.rem(b, 2)
    y, x_hi = lax.rem(r, 4), r // 4

    def block(offset):
        return (lax.rem(b + offset + n_blk, n_blk), r)

    def red(x_step, y_step):
        x_to = 1 - x_hi if x_step else x_hi
        return (b, x_to * 4 + lax.rem(y + y_step, 4))

    barrier = pltpu.get_barrier_semaphore()
    for offset in (-3, -2, -1, 1):
        pl.semaphore_signal(barrier, inc=1, device_id=block(offset), device_id_type=MESH)
    greets = ((y < 2, (0, 1)), (lax.rem(y, 3) == 0, (0, 3)), (x_hi == 0, (1, 0)))
    answers = ((y >= 2, (0, 1)), (lax.rem(y, 3) != 0, (0, 3)), (x_hi == 1, (1, 0)))
    greeted_by = lax.rem(y, 2) + 2 * (y // 2) * (1 - lax.rem(y, 2)) + x_hi

    def signal_where(sem, table):
        for holds, steps in table:
            @pl.when(holds)
            def _(steps=steps):
                pl.semaphore_signal(sem, inc=1, device_id=red(*steps), device_id_type=MESH)

    signal_where(barrier, greets)

    def label_copy(m):
        return pltpu.make_async_remote_copy(
            src_ref=labels.at[0], dst_ref=labels.at[m],
            send_sem=label_send, recv_sem=label_recv.at[m - 1],
            device_id=block(m), device_id_type=MESH,
        )

    def chunk(m, h, q):
        return slabs.at[2 * m + h, pl.ds(*CUTS[q])]

    def half_copy(h, q):
        return pltpu.make_async_remote_copy(
            src_ref=chunk(0, h, q), dst_ref=chunk(2 + h - c, h, q),
            send_sem=slab_send, recv_sem=half_recv.at[1 - c, q],
            device_id=block(2 + h - c), device_id_type=MESH,
        )

    def send_half(h):
        for q in range(2):
            half_copy(h, q).start()

    own_copy = pltpu.make_async_remote_copy(
        src_ref=slabs.at[pl.ds(0, 2)], dst_ref=slabs.at[pl.ds(2 + 4 * c, 2)],
        send_sem=slab_send, recv_sem=own_recv,
        device_id=block(1 + 2 * c), device_id_type=MESH,
    )
    loads[0].wait()
    loads[3].start()
    pair_columns = [column_of(labels[0, :, 128 * h : 128 * h + 128]) for h in range(2)]
    loads[1].wait()
    cd_labels = cd[...].astype(F32)
    for h in range(2):
        loads[2 + h].wait()
        if h == 1:
            loads[4].start()
            loads[5].start()
        tails = []
        for part in range(2):
            own = pair_columns[h][64 * part : 64 * part + 64]
            head, tail = folded(amp, 128 * h + 64 * part, 64, own, cd_labels)
            slabs[h, 64 * part : 64 * part + 64] = head
            tails.append(tail)
        slabs[h, 128:192] = jnp.where(lanes_below(64), *tails)
        if h == 0:
            pl.semaphore_wait(barrier, 4 + greeted_by)
            for m in (1, 2, 3):
                label_copy(m).start()

        @pl.when(k != 2)
        def _(h=h):
            send_half(h)

    @pl.when(k != 3)
    def _():
        own_copy.start()

    signal_where(reply_sem, answers)

    def forward(i, q):
        return pltpu.make_async_remote_copy(
            src_ref=chunk(1 + i + c, c, q), dst_ref=chunk(2 + i - c, c, q),
            send_sem=slab_send, recv_sem=fwd_recv.at[i],
            device_id=block(1 - 2 * c), device_id_type=MESH,
        )

    def forwarded(i):
        pltpu.make_async_remote_copy(
            src_ref=slabs.at[0], dst_ref=slabs.at[0],
            send_sem=slab_send, recv_sem=fwd_recv.at[i],
            device_id=block(1 - 2 * c), device_id_type=MESH,
        ).wait_recv()

    def pass_on(q):
        return pltpu.make_async_remote_copy(
            src_ref=chunk(1 + c, c, q), dst_ref=chunk(3, c, q),
            send_sem=slab_send, recv_sem=pass_recv,
            device_id=block(2 - c), device_id_type=MESH,
        )

    def all_slab_copies(halves):
        return pltpu.make_async_remote_copy(
            src_ref=slabs.at[pl.ds(0, halves)], dst_ref=slabs.at[pl.ds(0, halves)],
            send_sem=slab_send, recv_sem=pass_recv,
            device_id=block(2), device_id_type=MESH,
        )

    def half_arrival(i, q):
        return pltpu.make_async_remote_copy(
            src_ref=chunk(0, c, q), dst_ref=chunk(1 + i + c, c, q),
            send_sem=slab_send, recv_sem=half_recv.at[i, q],
            device_id=block(2), device_id_type=MESH,
        )

    def from_last_chip(i, hand_on=False):
        for q in range(2):
            half_arrival(i, q).wait_recv()
            if hand_on:
                pass_on(q).start()
            forward(i, q).start()

    loads[4].wait()
    loads[5].wait()

    @pl.when(k == 2)
    def _():
        send_half(0)
        send_half(1)

    for h in range(2):
        own = column_of(ab[:, 128 * h : 128 * h + 128])
        ab_col[128 * h : 128 * h + 128] = own
        for part in range(2):
            row = 128 * h + 64 * part
            head, tail = folded(integ, row, 64, own[64 * part : 64 * part + 64], cd_labels)
            for t, piece in enumerate((head, jnp.where(lanes_below(64), tail, 0.0))):
                high, low = split(piece)
                for place, value in ((t, high), (t + 2, low), (t + 4, high)):
                    v_parts[row : row + 64, place * LANES : (place + 1) * LANES] = value

    def dot(lhs, rhs):
        return lax.dot_general(lhs, rhs, (((1,), (1,)), ((), ())), preferred_element_type=F32)

    def to_peers(m):
        for x_step in (1, 0):
            for y_step in (2, 1, 3, 0):
                if x_step or y_step:
                    to = red(x_step, y_step)
                    pltpu.make_async_remote_copy(
                        src_ref=send.at[m, to[1]], dst_ref=arrived.at[m, 4 * x_step + y_step - 1],
                        send_sem=red_send, recv_sem=red_recv.at[m],
                        device_id=to, device_id_type=MESH,
                    ).start()

    def all_peers(m):
        return pltpu.make_async_remote_copy(
            src_ref=arrived.at[m], dst_ref=arrived.at[m],
            send_sem=red_send, recv_sem=red_recv.at[m],
            device_id=red(1, 0), device_id_type=MESH,
        )

    def process(m):
        parts = []
        for h in range(2):
            tail = slabs[2 * m + h, 128:192]
            parts.append(jnp.concatenate([slabs[2 * m + h, 0:64], tail], axis=1))
            parts.append(jnp.concatenate([slabs[2 * m + h, 64:128], pltpu.roll(tail, 64, 1)], axis=1))
        high, rest = split(jnp.concatenate(parts, axis=0))
        product = dot(v_parts[...], jnp.concatenate([high, high, rest], axis=1))
        masked = jnp.zeros((256, LANES), F32)
        for h in range(2):
            mask = ab_col[...] == labels[m, :, 128 * h : 128 * h + 128].astype(F32)
            masked = masked + jnp.where(mask, product[:, 128 * h : 128 * h + 128], 0.0)
        twice = masked + pltpu.roll(masked, 64, 1)
        low = lanes_below(16)
        for block_row in range(8):
            row = 32 * block_row
            send[m, block_row] = jnp.where(low, twice[row : row + 16], twice[row + 16 : row + 32])

    def finish(m):
        all_peers(m).wait_recv()
        total = send[m, r]
        for i in range(7):
            total = total + arrived[m, i]
        turned = pltpu.roll(total, 64, 1)
        low = lanes_below(16)
        rows = jnp.concatenate([jnp.where(low, total, turned), jnp.where(low, turned, total)], axis=0)
        own = ab_col[pl.ds(pl.multiple_of(32 * r, 32), 32)]
        for h in range(2):
            mask = own == labels[m, :, 128 * h : 128 * h + 128].astype(F32)
            out_ref[m, :, 128 * h : 128 * h + 128] = jnp.where(mask, rows, 0.0)

    first, second, third = 3 - 2 * c, 1 + c, 2 + c

    def shift(m):
        label_copy(m).wait_recv()
        process(m)
        to_peers(m)

    process(0)

    @pl.when(greeted_by < 3)
    def _():
        pl.semaphore_wait(reply_sem, 3 - greeted_by)

    for steps in NEAR:
        pl.semaphore_signal(near_sem, inc=1, device_id=red(*steps), device_id_type=MESH)

    @pl.when(k == 0)
    def _():
        from_last_chip(0, hand_on=True)

    pl.semaphore_wait(near_sem, 3)
    pl.semaphore_signal(far_sem, inc=1, device_id=red(0, 3), device_id_type=MESH)

    @pl.when(k != 0)
    def _():
        pl.semaphore_wait(far_sem, 1)
        to_peers(0)

    @pl.when(k == 0)
    def _():
        own_copy.wait_recv()
        label_copy(3).wait_recv()
        process(3)
        from_last_chip(1)
        pl.semaphore_wait(far_sem, 1)
        to_peers(0)
        to_peers(3)
        forwarded(0)
        shift(1)
        forwarded(1)
        shift(2)
        finish(0)
        finish(3)
        finish(1)
        finish(2)

    @pl.when(k == 2)
    def _():
        from_last_chip(0)
        from_last_chip(1)
        forwarded(0)
        shift(1)
        forwarded(1)
        shift(2)
        finish(0)
        all_slab_copies(2).wait_recv()
        shift(3)
        finish(1)
        finish(2)
        finish(3)

    @pl.when(c == 1)
    def _():
        own_copy.wait_recv()
        shift(1)

        @pl.when(k == 1)
        def _():
            from_last_chip(0, hand_on=True)

        @pl.when(k == 3)
        def _():
            from_last_chip(0)

        forwarded(0)
        shift(2)
        from_last_chip(1)
        forwarded(1)
        shift(3)
        finish(0)
        finish(1)
        finish(2)
        finish(3)

    for halves, blocks in ((7, k < 2), (6, k == 2), (4, k == 3)):
        @pl.when(blocks)
        def _(halves=halves):
            all_slab_copies(halves).wait_send()

    pltpu.make_async_remote_copy(
        src_ref=labels.at[pl.ds(1, 3)], dst_ref=labels.at[pl.ds(1, 3)],
        send_sem=label_send, recv_sem=label_recv.at[0],
        device_id=block(1), device_id_type=MESH,
    ).wait_send()
    pltpu.make_async_remote_copy(
        src_ref=arrived, dst_ref=arrived,
        send_sem=red_send, recv_sem=red_recv.at[0],
        device_id=red(1, 0), device_id_type=MESH,
    ).wait_send()


def solution(mesh):
    n_blk = mesh.shape["blk"]

    def body(amplitudes, integrals, cd_irrep, ab_irrep, ij_irrep):
        vmem = pl.BlockSpec(memory_space=pltpu.VMEM)
        hbm = pl.BlockSpec(memory_space=pltpu.HBM)
        return pl.pallas_call(
            functools.partial(kernel, n_blk),
            out_shape=pltpu.VMEM((SHIFTS, 32, 256), F32),
            in_specs=[hbm] * 5,
            out_specs=vmem,
            scratch_shapes=[
                pltpu.VMEM((256, 768), F32),
                pltpu.VMEM((256, 768), F32),
                pltpu.VMEM((1, 768), jnp.int32),
                pltpu.VMEM((1, 256), jnp.int32),
                pltpu.VMEM((SHIFTS, 1, 256), jnp.int32),
                pltpu.VMEM((2 * SHIFTS, HALF, LANES), F32),
                pltpu.VMEM((256, 768), BF16),
                pltpu.VMEM((256, LANES), F32),
                pltpu.VMEM((SHIFTS, 8, 16, LANES), F32),
                pltpu.VMEM((SHIFTS, 7, 16, LANES), F32),
                pltpu.SemaphoreType.DMA((6,)),
                pltpu.SemaphoreType.REGULAR,
                pltpu.SemaphoreType.REGULAR,
                pltpu.SemaphoreType.REGULAR,
                pltpu.SemaphoreType.DMA,
                pltpu.SemaphoreType.DMA((3,)),
                pltpu.SemaphoreType.DMA,
                pltpu.SemaphoreType.DMA,
                pltpu.SemaphoreType.DMA((2, 2)),
                pltpu.SemaphoreType.DMA((2,)),
                pltpu.SemaphoreType.DMA,
                pltpu.SemaphoreType.DMA,
                pltpu.SemaphoreType.DMA((SHIFTS,)),
            ],
            compiler_params=pltpu.CompilerParams(
                collective_id=0, has_side_effects=True, vmem_limit_bytes=VMEM_LIMIT
            ),
        )(amplitudes, integrals, cd_irrep, ab_irrep, ij_irrep)

    in_specs = (P("blk", "red"), P("blk", "red"), P("red", None), P("blk", None), P("blk", None))
    out_specs = P(None, ("blk", "red"), None)
    return jax.shard_map(body, mesh=mesh, in_specs=in_specs, out_specs=out_specs, check_vma=False)
```

```python
import functools

import jax
import jax.numpy as jnp
from jax import lax
from jax.experimental import pallas as pl
from jax.experimental.pallas import tpu as pltpu
from jax.sharding import PartitionSpec as P

SHIFTS = 4
MESH = pl.DeviceIdType.MESH
F32 = jnp.float32
BF16 = jnp.bfloat16
LANES = 128
NEAR = ((0, 1), (0, 3), (1, 0))
VMEM_LIMIT = 60 * 1024 * 1024
CUTS = ((0, 96), (96, 96))
HALF = 192


def lanes_below(rows):
    return lax.broadcasted_iota(jnp.int32, (rows, LANES), 1) < 64


def column_of(labels):
    return jnp.transpose(jnp.broadcast_to(labels.astype(F32), (LANES, LANES)))


def folded(ref, row, rows, own, cd_labels):
    def kept(t):
        value = ref[pl.ds(row, rows), t * LANES : (t + 1) * LANES]
        return jnp.where(own == cd_labels[:, t * LANES : (t + 1) * LANES], value, 0.0)

    f0, f1, f2 = (kept(t) + kept(t + 3) for t in range(3))
    low = lanes_below(rows)
    head = f0 + pltpu.roll(jnp.where(low, f2, f1), 64, 1)
    tail = jnp.where(low, f1, f2)
    return head, tail + pltpu.roll(tail, 64, 1)


def split(value):
    high = value.astype(BF16)
    return high, (value - high.astype(F32)).astype(BF16)


def kernel(
    n_blk, amp_hbm, int_hbm, cd_hbm, ab_hbm, ij_hbm, out_ref,
    amp, integ, cd, ab, labels, slabs, v_parts, ab_col, send, arrived,
    load_sem, near_sem, far_sem, label_send, label_recv, slab_send, own_recv, half_recv, fwd_recv, pass_recv,
    red_send, red_recv,
):
    loads = [
        pltpu.make_async_copy(src, dst, load_sem.at[i])
        for i, (src, dst) in enumerate((
            (ij_hbm, labels.at[0]),
            (cd_hbm, cd),
            (amp_hbm.at[pl.ds(0, 128)], amp.at[pl.ds(0, 128)]),
            (amp_hbm.at[pl.ds(128, 128)], amp.at[pl.ds(128, 128)]),
            (ab_hbm, ab),
            (int_hbm, integ),
        ))
    ]
    for load in loads[:4]:
        load.start()

    b, r = lax.axis_index("blk"), lax.axis_index("red")
    k = lax.rem(b, 4)
    c = lax.rem(b, 2)
    y, x_hi = lax.rem(r, 4), r // 4

    def block(offset):
        return (lax.rem(b + offset + n_blk, n_blk), r)

    def red(x_step, y_step):
        x_to = 1 - x_hi if x_step else x_hi
        return (b, x_to * 4 + lax.rem(y + y_step, 4))

    barrier = pltpu.get_barrier_semaphore()
    for offset in (-3, -2, -1, 1):
        pl.semaphore_signal(barrier, inc=1, device_id=block(offset), device_id_type=MESH)
    for steps in NEAR:
        pl.semaphore_signal(barrier, inc=1, device_id=red(*steps), device_id_type=MESH)

    def label_copy(m):
        return pltpu.make_async_remote_copy(
            src_ref=labels.at[0], dst_ref=labels.at[m],
            send_sem=label_send, recv_sem=label_recv.at[m - 1],
            device_id=block(m), device_id_type=MESH,
        )

    def chunk(m, h, q):
        return slabs.at[2 * m + h, pl.ds(*CUTS[q])]

    def half_copy(h, q):
        return pltpu.make_async_remote_copy(
            src_ref=chunk(0, h, q), dst_ref=chunk(2 + h - c, h, q),
            send_sem=slab_send, recv_sem=half_recv.at[1 - c, q],
            device_id=block(2 + h - c), device_id_type=MESH,
        )

    def send_half(h):
        for q in range(2):
            half_copy(h, q).start()

    own_copy = pltpu.make_async_remote_copy(
        src_ref=slabs.at[pl.ds(0, 2)], dst_ref=slabs.at[pl.ds(2 + 4 * c, 2)],
        send_sem=slab_send, recv_sem=own_recv,
        device_id=block(1 + 2 * c), device_id_type=MESH,
    )
    loads[0].wait()
    pair_labels = [labels[0, :, 128 * h : 128 * h + 128] for h in range(2)]
    pair_columns = [column_of(row) for row in pair_labels]
    loads[1].wait()
    cd_labels = cd[...].astype(F32)
    loads[2].wait()
    for h in range(2):
        tails = []
        for part in range(2):
            own = pair_columns[h][64 * part : 64 * part + 64]
            head, tail = folded(amp, 128 * h + 64 * part, 64, own, cd_labels)
            slabs[h, 64 * part : 64 * part + 64] = head
            tails.append(tail)
        slabs[h, 128:192] = jnp.where(lanes_below(64), *tails)
        if h == 0:
            loads[3].wait()
            loads[4].start()
            loads[5].start()
            pl.semaphore_wait(barrier, 7)
            for m in (1, 2, 3):
                label_copy(m).start()

        @pl.when(k != 2)
        def _(h=h):
            send_half(h)

    @pl.when(k != 3)
    def _():
        own_copy.start()

    for steps in NEAR:
        pl.semaphore_signal(near_sem, inc=1, device_id=red(*steps), device_id_type=MESH)

    def forward(i, q):
        return pltpu.make_async_remote_copy(
            src_ref=chunk(1 + i + c, c, q), dst_ref=chunk(2 + i - c, c, q),
            send_sem=slab_send, recv_sem=fwd_recv.at[i],
            device_id=block(1 - 2 * c), device_id_type=MESH,
        )

    def forwarded(i):
        pltpu.make_async_remote_copy(
            src_ref=slabs.at[0], dst_ref=slabs.at[0],
            send_sem=slab_send, recv_sem=fwd_recv.at[i],
            device_id=block(1 - 2 * c), device_id_type=MESH,
        ).wait_recv()

    def pass_on(q):
        return pltpu.make_async_remote_copy(
            src_ref=chunk(1 + c, c, q), dst_ref=chunk(3, c, q),
            send_sem=slab_send, recv_sem=pass_recv,
            device_id=block(2 - c), device_id_type=MESH,
        )

    def all_slab_copies(halves):
        return pltpu.make_async_remote_copy(
            src_ref=slabs.at[pl.ds(0, halves)], dst_ref=slabs.at[pl.ds(0, halves)],
            send_sem=slab_send, recv_sem=pass_recv,
            device_id=block(2), device_id_type=MESH,
        )

    def half_arrival(i, q):
        return pltpu.make_async_remote_copy(
            src_ref=chunk(0, c, q), dst_ref=chunk(1 + i + c, c, q),
            send_sem=slab_send, recv_sem=half_recv.at[i, q],
            device_id=block(2), device_id_type=MESH,
        )

    def from_last_chip(i, hand_on=False):
        for q in range(2):
            half_arrival(i, q).wait_recv()
            if hand_on:
                pass_on(q).start()
            forward(i, q).start()

    loads[4].wait()
    loads[5].wait()
    for h in range(2):
        own = column_of(ab[:, 128 * h : 128 * h + 128])
        ab_col[128 * h : 128 * h + 128] = own
        for part in range(2):
            row = 128 * h + 64 * part
            head, tail = folded(integ, row, 64, own[64 * part : 64 * part + 64], cd_labels)
            for t, piece in enumerate((head, jnp.where(lanes_below(64), tail, 0.0))):
                high, low = split(piece)
                for place, value in ((t, high), (t + 2, low), (t + 4, high)):
                    v_parts[row : row + 64, place * LANES : (place + 1) * LANES] = value

    def dot(lhs, rhs):
        return lax.dot_general(lhs, rhs, (((1,), (1,)), ((), ())), preferred_element_type=F32)

    def to_peers(m):
        for x_step in (1, 0):
            for y_step in (2, 1, 3, 0):
                if x_step or y_step:
                    to = red(x_step, y_step)
                    pltpu.make_async_remote_copy(
                        src_ref=send.at[m, to[1]], dst_ref=arrived.at[m, 4 * x_step + y_step - 1],
                        send_sem=red_send, recv_sem=red_recv.at[m],
                        device_id=to, device_id_type=MESH,
                    ).start()

    def all_peers(m):
        return pltpu.make_async_remote_copy(
            src_ref=arrived.at[m], dst_ref=arrived.at[m],
            send_sem=red_send, recv_sem=red_recv.at[m],
            device_id=red(1, 0), device_id_type=MESH,
        )

    def process(m):
        parts = []
        for h in range(2):
            tail = slabs[2 * m + h, 128:192]
            parts.append(jnp.concatenate([slabs[2 * m + h, 0:64], tail], axis=1))
            parts.append(jnp.concatenate([slabs[2 * m + h, 64:128], pltpu.roll(tail, 64, 1)], axis=1))
        high, rest = split(jnp.concatenate(parts, axis=0))
        product = dot(v_parts[...], jnp.concatenate([high, high, rest], axis=1))
        masked = jnp.zeros((256, LANES), F32)
        for h in range(2):
            mask = ab_col[...] == labels[m, :, 128 * h : 128 * h + 128].astype(F32)
            masked = masked + jnp.where(mask, product[:, 128 * h : 128 * h + 128], 0.0)
        twice = masked + pltpu.roll(masked, 64, 1)
        low = lanes_below(16)
        for block_row in range(8):
            row = 32 * block_row
            send[m, block_row] = jnp.where(low, twice[row : row + 16], twice[row + 16 : row + 32])

    def finish(m):
        all_peers(m).wait_recv()
        total = send[m, r]
        for i in range(7):
            total = total + arrived[m, i]
        turned = pltpu.roll(total, 64, 1)
        low = lanes_below(16)
        rows = jnp.concatenate([jnp.where(low, total, turned), jnp.where(low, turned, total)], axis=0)
        own = ab_col[pl.ds(pl.multiple_of(32 * r, 32), 32)]
        for h in range(2):
            mask = own == labels[m, :, 128 * h : 128 * h + 128].astype(F32)
            out_ref[m, :, 128 * h : 128 * h + 128] = jnp.where(mask, rows, 0.0)

    first, second, third = 3 - 2 * c, 1 + c, 2 + c

    def shift(m):
        label_copy(m).wait_recv()
        process(m)
        to_peers(m)

    process(0)

    @pl.when(k == 2)
    def _():
        send_half(0)
        send_half(1)

    pl.semaphore_wait(near_sem, 3)
    pl.semaphore_signal(far_sem, inc=1, device_id=red(0, 3), device_id_type=MESH)

    @pl.when(k == 0)
    def _():
        from_last_chip(0, hand_on=True)

    pl.semaphore_wait(far_sem, 1)
    to_peers(0)

    @pl.when(k == 0)
    def _():
        own_copy.wait_recv()
        shift(3)
        from_last_chip(1)
        forwarded(0)
        shift(1)
        forwarded(1)
        shift(2)
        finish(0)
        finish(3)
        finish(1)
        finish(2)

    @pl.when(k == 2)
    def _():
        from_last_chip(0)
        from_last_chip(1)
        forwarded(0)
        shift(1)
        forwarded(1)
        shift(2)
        finish(0)
        all_slab_copies(2).wait_recv()
        shift(3)
        finish(1)
        finish(2)
        finish(3)

    @pl.when(c == 1)
    def _():
        own_copy.wait_recv()
        shift(1)

        @pl.when(k == 1)
        def _():
            from_last_chip(0, hand_on=True)

        @pl.when(k == 3)
        def _():
            from_last_chip(0)

        forwarded(0)
        shift(2)
        from_last_chip(1)
        forwarded(1)
        shift(3)
        finish(0)
        finish(1)
        finish(2)
        finish(3)

    for halves, blocks in ((7, k < 2), (6, k == 2), (4, k == 3)):
        @pl.when(blocks)
        def _(halves=halves):
            all_slab_copies(halves).wait_send()

    pltpu.make_async_remote_copy(
        src_ref=labels.at[pl.ds(1, 3)], dst_ref=labels.at[pl.ds(1, 3)],
        send_sem=label_send, recv_sem=label_recv.at[0],
        device_id=block(1), device_id_type=MESH,
    ).wait_send()
    pltpu.make_async_remote_copy(
        src_ref=arrived, dst_ref=arrived,
        send_sem=red_send, recv_sem=red_recv.at[0],
        device_id=red(1, 0), device_id_type=MESH,
    ).wait_send()


def solution(mesh):
    n_blk = mesh.shape["blk"]

    def body(amplitudes, integrals, cd_irrep, ab_irrep, ij_irrep):
        vmem = pl.BlockSpec(memory_space=pltpu.VMEM)
        hbm = pl.BlockSpec(memory_space=pltpu.HBM)
        return pl.pallas_call(
            functools.partial(kernel, n_blk),
            out_shape=pltpu.VMEM((SHIFTS, 32, 256), F32),
            in_specs=[hbm] * 5,
            out_specs=vmem,
            scratch_shapes=[
                pltpu.VMEM((256, 768), F32),
                pltpu.VMEM((256, 768), F32),
                pltpu.VMEM((1, 768), jnp.int32),
                pltpu.VMEM((1, 256), jnp.int32),
                pltpu.VMEM((SHIFTS, 1, 256), jnp.int32),
                pltpu.VMEM((2 * SHIFTS, HALF, LANES), F32),
                pltpu.VMEM((256, 768), BF16),
                pltpu.VMEM((256, LANES), F32),
                pltpu.VMEM((SHIFTS, 8, 16, LANES), F32),
                pltpu.VMEM((SHIFTS, 7, 16, LANES), F32),
                pltpu.SemaphoreType.DMA((6,)),
                pltpu.SemaphoreType.REGULAR,
                pltpu.SemaphoreType.REGULAR,
                pltpu.SemaphoreType.DMA,
                pltpu.SemaphoreType.DMA((3,)),
                pltpu.SemaphoreType.DMA,
                pltpu.SemaphoreType.DMA,
                pltpu.SemaphoreType.DMA((2, 2)),
                pltpu.SemaphoreType.DMA((2,)),
                pltpu.SemaphoreType.DMA,
                pltpu.SemaphoreType.DMA,
                pltpu.SemaphoreType.DMA((SHIFTS,)),
            ],
            compiler_params=pltpu.CompilerParams(
                collective_id=0, has_side_effects=True, vmem_limit_bytes=VMEM_LIMIT
            ),
        )(amplitudes, integrals, cd_irrep, ab_irrep, ij_irrep)

    in_specs = (P("blk", "red"), P("blk", "red"), P("red", None), P("blk", None), P("blk", None))
    out_specs = P(None, ("blk", "red"), None)
    return jax.shard_map(body, mesh=mesh, in_specs=in_specs, out_specs=out_specs, check_vma=False)
```
